32 devices in a mesh: depth: 4 (over z), lat: 8 (over y, x, core).
Axes of the slice: x: 2, y: 2, z: 4, core: 2. Of those that a mesh axis runs over, the one named last changes fastest.
Arguments:
- down_real: float32 [16, 256, 256], P('depth', 'lat'), may hold values from -6 to 6
- down_imaginary: float32 [16, 256, 256], P('depth', 'lat'), may hold values from -6 to 6
- up_real: float32 [16, 256, 256], P('depth', 'lat'), may hold values from -6 to 6
- up_imaginary: float32 [16, 256, 256], P('depth', 'lat'), may hold values from -6 to 6
- slowness: float32 [16, 256, 256], P('depth', 'lat'), may hold values from 0.7 to 1.4
- ref_slow: float32 [16], P('depth'), may hold values from 0.8 to 1.2
- reflectivity: float32 [16, 256, 256], P('depth', 'lat'), may hold values from -0.3 to 0.3
- source_real: float32 [256, 256], P('lat'), may hold values from -6 to 6
- source_imaginary: float32 [256, 256], P('lat'), may hold values from -6 to 6
Outputs:
- next_down_real: float32 [16, 256, 256], P('depth', 'lat')
- next_down_imaginary: float32 [16, 256, 256], P('depth', 'lat')
- next_up_real: float32 [16, 256, 256], P('depth', 'lat')
- next_up_imaginary: float32 [16, 256, 256], P('depth', 'lat')
The draws below stay inside these ranges and needn't reach their ends.
All inputs are finite; a program needn't handle non-finite values.
Results may differ from the reference program's by a relative error of at most 0.0003.
Values sent between devices are 32-bit elements; how exact they have to be, the bound alone decides.
No kernel may reach another device: no remote copies, remote signals or barrier semaphores. Data moves between devices by JAX's collectives and lax.ppermute only.
A program may use at most 64 MiB of HBM per device.

```python
import math
import jax
import jax.numpy as jnp
from jax import lax

NX = 256
NY = 256
TICKS = 3
NZ = 16


def block_levels(stream_key, dims, pieces, low, high):
    gain, own = 1.0, jax.random.fold_in(stream_key, 6)
    for dim, parts in pieces:
        steps = jnp.exp(jax.random.uniform(jax.random.fold_in(own, dim), (parts,), jnp.float32, low / len(pieces), high / len(pieces)))
        gain = gain * jnp.repeat(steps, dims[dim] // parts).reshape([-1 if axis == dim else 1 for axis in range(len(dims))])
    return gain


def bell_draw(stream_key, dims, spread, bound, cuts=(), kind=jnp.bfloat16):
    result = spread * jax.random.normal(stream_key, dims, jnp.float32)
    if cuts:
        result = result * block_levels(stream_key, dims, cuts, -0.22, 0.18)
    return jnp.clip(result, -bound, bound).astype(kind)


def setup_inputs(seed: int = 0) -> dict:
    key_list = jax.random.split(jax.random.key(seed), 10)
    return {
        "down_real": bell_draw(key_list[0], (NZ, NX, NY), 1.0, 6.0, ((0, 4), (1, 8)), jnp.float32),
        "down_imaginary": bell_draw(key_list[1], (NZ, NX, NY), 1.0, 6.0, ((0, 4), (1, 8)), jnp.float32),
        "up_real": bell_draw(key_list[2], (NZ, NX, NY), 1.0, 6.0, ((0, 4), (1, 8)), jnp.float32),
        "up_imaginary": bell_draw(key_list[3], (NZ, NX, NY), 1.0, 6.0, ((0, 4), (1, 8)), jnp.float32),
        "slowness": jnp.clip(0.7 + 0.7 * jax.random.uniform(key_list[4], (NZ, NX, NY), jnp.float32) ** block_levels(key_list[4], (NZ, NX, NY), ((0, 4), (1, 8)), -0.2, 0.2), 0.7, 1.4),
        "ref_slow": jnp.clip(0.8 + 0.40000004 * jax.random.uniform(key_list[5], (NZ,), jnp.float32) ** block_levels(key_list[5], (NZ,), ((0, 4),), -0.2, 0.2), 0.8, 1.2),
        "reflectivity": jnp.clip(jax.random.uniform(key_list[6], (NZ, NX, NY), jnp.float32, -0.3, 0.3) * block_levels(key_list[6], (NZ, NX, NY), ((0, 4), (1, 8)), -0.4, 0.0), -0.3, 0.3),
        "source_real": bell_draw(key_list[7], (NX, NY), 1.0, 6.0, ((0, 8),), jnp.float32),
        "source_imaginary": bell_draw(key_list[8], (NX, NY), 1.0, 6.0, ((0, 8),), jnp.float32),
    }


OMEGA = 2.5
DEPTH_STEP = 1.0

def wavenumbers(count):
    index = jnp.arange(count, dtype=jnp.int32)
    wrapped = jnp.where(index < count // 2, index, index - count)
    return wrapped.astype(jnp.float32) * (2.0 * math.pi / count)

def propagate(real, imag, slowness, ref_slow):
    wave_x = wavenumbers(NX)
    wave_y = wavenumbers(NY)
    squared = wave_x[:, None] ** 2 + wave_y[None, :] ** 2

    def one_level(items):
        plane_real, plane_imag, slow_plane, slow_ref = items
        plane = plane_real + 1j * plane_imag
        spectrum = jnp.fft.fft2(plane)
        argument = (OMEGA * slow_ref) ** 2 - squared
        vertical = jnp.sqrt(jnp.maximum(argument, 0.0)) * DEPTH_STEP
        evanescent = jnp.sqrt(jnp.maximum(-argument, 0.0)) * DEPTH_STEP
        factor = jnp.exp(-evanescent)
        multiplier = factor * jnp.cos(vertical) - 1j * (factor * jnp.sin(vertical))
        shifted = jnp.fft.ifft2(spectrum * multiplier)
        theta = OMEGA * (slow_plane - slow_ref) * DEPTH_STEP
        corrected = shifted * (jnp.cos(theta) - 1j * jnp.sin(theta))
        return (jnp.real(corrected), jnp.imag(corrected))
    return lax.map(one_level, (real, imag, slowness, ref_slow))

def reference(down_real, down_imaginary, up_real, up_imaginary, slowness, ref_slow, reflectivity, source_real, source_imaginary):
    for tick in range(TICKS):
        prop_down_real, prop_down_imag = propagate(down_real, down_imaginary, slowness, ref_slow)
        prop_up_real, prop_up_imag = propagate(up_real, up_imaginary, slowness, ref_slow)
        in_down_real = jnp.concatenate([source_real[None], prop_down_real[:-1]], axis=0)
        in_down_imag = jnp.concatenate([source_imaginary[None], prop_down_imag[:-1]], axis=0)
        in_up_real = jnp.concatenate([prop_up_real[1:], jnp.zeros_like(prop_up_real[:1])], axis=0)
        in_up_imag = jnp.concatenate([prop_up_imag[1:], jnp.zeros_like(prop_up_imag[:1])], axis=0)
        down_real = in_down_real - reflectivity * in_up_real
        down_imaginary = in_down_imag - reflectivity * in_up_imag
        up_real = in_up_real + reflectivity * in_down_real
        up_imaginary = in_up_imag + reflectivity * in_down_imag
    return (down_real, down_imaginary, up_real, up_imaginary)
```

```python
import math

import jax
import jax.numpy as jnp
import numpy as np
from jax import lax
from jax.experimental import pallas as pl
from jax.experimental.pallas import tpu as pltpu
from jax.sharding import PartitionSpec as P

TICKS = 3


OMEGA = 2.5
DEPTH_STEP = 1.0


def passed_along(value, axis, steps):
    count = lax.axis_size(axis)
    initial, last = (max(0, -steps), min(count, count - steps))
    return lax.ppermute(value, axis, [(source, source + steps) for source in range(initial, last)])


def tables(count):
    index = jnp.arange(count, dtype=jnp.int32)
    phase = index[:, None] * index[None, :] % count
    angle = phase.astype(jnp.float32) * (2.0 * math.pi / count)
    return (jnp.cos(angle), jnp.sin(angle))


def wrapped_numbers(index, count):
    folded = jnp.where(index < count // 2, index, index - count)
    return folded.astype(jnp.float32) * (2.0 * math.pi / count)


def complex_product(form, real, imag, cosine, sine, inverse):
    real_cos = jnp.einsum(form, real, cosine, precision=lax.Precision.HIGHEST)
    real_sin = jnp.einsum(form, real, sine, precision=lax.Precision.HIGHEST)
    imag_cos = jnp.einsum(form, imag, cosine, precision=lax.Precision.HIGHEST)
    imag_sin = jnp.einsum(form, imag, sine, precision=lax.Precision.HIGHEST)
    if inverse:
        return (real_cos - imag_sin, imag_cos + real_sin)
    return (real_cos + imag_sin, imag_cos - real_sin)


def spectral(real, imag, mult_real, mult_imag, corr_real, corr_imag, all_tables, lat_count):
    cos_y, sin_y, cos_x, sin_x = all_tables
    planes = real.shape[0]
    rows_here = real.shape[1]
    width_y = real.shape[2]
    width_x = rows_here * lat_count
    cols_here = width_y // lat_count
    first_real, first_imag = complex_product("nxy,yk->xkn", real, imag, cos_y, sin_y, False)
    send_real = jnp.swapaxes(
        first_real.reshape(rows_here, lat_count, cols_here, planes), 0, 1
    ).reshape(lat_count, rows_here * cols_here * planes)
    send_imag = jnp.swapaxes(
        first_imag.reshape(rows_here, lat_count, cols_here, planes), 0, 1
    ).reshape(lat_count, rows_here * cols_here * planes)
    got_real, got_imag = (
        lax.all_to_all(send_real, "lat", split_axis=0, concat_axis=0, tiled=True),
        lax.all_to_all(send_imag, "lat", split_axis=0, concat_axis=0, tiled=True),
    )
    got_real = got_real.reshape(width_x, cols_here, planes)
    got_imag = got_imag.reshape(width_x, cols_here, planes)
    spec_real, spec_imag = complex_product("xqn,xp->nqp", got_real, got_imag, cos_x, sin_x, False)
    moved_real = spec_real * mult_real - spec_imag * mult_imag
    moved_imag = spec_real * mult_imag + spec_imag * mult_real
    back_real, back_imag = complex_product(
        "nqp,px->qxn", moved_real, moved_imag, cos_x, sin_x, True
    )
    back_real = jnp.swapaxes(
        (back_real / width_x).reshape(cols_here, lat_count, rows_here, planes), 0, 1
    ).reshape(lat_count, cols_here * rows_here * planes)
    back_imag = jnp.swapaxes(
        (back_imag / width_x).reshape(cols_here, lat_count, rows_here, planes), 0, 1
    ).reshape(lat_count, cols_here * rows_here * planes)
    ret_real, ret_imag = (
        lax.all_to_all(back_real, "lat", split_axis=0, concat_axis=0, tiled=True),
        lax.all_to_all(back_imag, "lat", split_axis=0, concat_axis=0, tiled=True),
    )
    ret_real = ret_real.reshape(width_y, rows_here, planes)
    ret_imag = ret_imag.reshape(width_y, rows_here, planes)
    plane_real, plane_imag = complex_product("kxn,ky->nxy", ret_real, ret_imag, cos_y, sin_y, True)
    plane_real = plane_real / width_y
    plane_imag = plane_imag / width_y
    final_real = plane_real * corr_real - plane_imag * corr_imag
    final_imag = plane_real * corr_imag + plane_imag * corr_real
    return (final_real, final_imag)


def media_factors(slow_planes, slow_refs, lat_count, lat_index):
    rows_here = slow_planes.shape[1]
    width_y = slow_planes.shape[2]
    width_x = rows_here * lat_count
    cols_here = width_y // lat_count
    wave_x = wrapped_numbers(jnp.arange(width_x, dtype=jnp.int32), width_x)
    wave_y = wrapped_numbers(
        lat_index * cols_here + jnp.arange(cols_here, dtype=jnp.int32), width_y
    )
    squared = wave_y[:, None] ** 2 + wave_x[None, :] ** 2
    argument = (OMEGA * slow_refs[:, None, None]) ** 2 - squared[None]
    vertical = jnp.sqrt(jnp.maximum(argument, 0.0)) * DEPTH_STEP
    evanescent = jnp.sqrt(jnp.maximum(-argument, 0.0)) * DEPTH_STEP
    factor = jnp.exp(-evanescent)
    theta = OMEGA * (slow_planes - slow_refs[:, None, None]) * DEPTH_STEP
    return (
        factor * jnp.cos(vertical),
        -factor * jnp.sin(vertical),
        jnp.cos(theta),
        -jnp.sin(theta),
    )


def row_shards(
    down_real,
    down_imaginary,
    up_real,
    up_imaginary,
    slowness,
    ref_slow,
    reflectivity,
    source_real,
    source_imaginary,
):
    levels = down_real.shape[0]
    lat_count = lax.axis_size("lat")
    lat_index = lax.axis_index("lat")
    top_mask = (lax.axis_index("depth") == 0).astype(jnp.float32)
    width_x = down_real.shape[1] * lat_count
    cos_y, sin_y = tables(down_real.shape[2])
    cos_x, sin_x = tables(width_x)
    all_tables = (cos_y, sin_y, cos_x, sin_x)
    slow_planes = jnp.concatenate([slowness, slowness], axis=0)
    slow_refs = jnp.concatenate([ref_slow, ref_slow], axis=0)
    mult_real, mult_imag, corr_real, corr_imag = media_factors(
        slow_planes, slow_refs, lat_count, lat_index
    )
    for tick in range(TICKS):
        joined_real = jnp.concatenate([down_real, up_real], axis=0)
        joined_imag = jnp.concatenate([down_imaginary, up_imaginary], axis=0)
        prop_real, prop_imag = spectral(
            joined_real,
            joined_imag,
            mult_real,
            mult_imag,
            corr_real,
            corr_imag,
            all_tables,
            lat_count,
        )
        above_real, above_imag = passed_along(
            (prop_real[levels - 1], prop_imag[levels - 1]), "depth", 1
        )
        below_real, below_imag = passed_along((prop_real[levels], prop_imag[levels]), "depth", -1)
        head_real = above_real + top_mask * source_real
        head_imag = above_imag + top_mask * source_imaginary
        in_down_real = jnp.concatenate([head_real[None], prop_real[: levels - 1]], axis=0)
        in_down_imag = jnp.concatenate([head_imag[None], prop_imag[: levels - 1]], axis=0)
        in_up_real = jnp.concatenate([prop_real[levels + 1 :], below_real[None]], axis=0)
        in_up_imag = jnp.concatenate([prop_imag[levels + 1 :], below_imag[None]], axis=0)
        down_real = in_down_real - reflectivity * in_up_real
        down_imaginary = in_down_imag - reflectivity * in_up_imag
        up_real = in_up_real + reflectivity * in_down_real
        up_imaginary = in_up_imag + reflectivity * in_down_imag
    return (down_real, down_imaginary, up_real, up_imaginary)


def path_at(section, place, pairs):
    place = place if section % 2 == 0 else pairs - 1 - place
    return place ^ (place >> 1)


def place_on(section, pair, pairs):
    shift, place = 1, pair
    while (1 << shift) <= pairs:
        place = place ^ (pair >> shift)
        shift += 1
    return jnp.where(section % 2 == 0, place, pairs - 1 - place)


def entry_pairs(step, sections, pairs):
    edges = []
    inverse = [{path_at(g, l, pairs): l for l in range(pairs)} for g in range(sections)]

    def device(g, c, core):
        return g * pairs * 2 + c * 2 + core

    for g in range(sections):
        for c in range(pairs):
            place = inverse[g][c ^ step]
            if place >= 1:
                edges.append((device(g, c, 0), device(g, c ^ step, 0)))
            elif g + 1 < sections:
                edges.append((device(g, c, 0), device(g + 1, path_at(g + 1, 0, pairs), 0)))
            if place < pairs - 1:
                edges.append((device(g, c, 1), device(g, c ^ step, 1)))
            elif g > 0:
                edges.append((device(g, c, 1), device(g - 1, path_at(g - 1, pairs - 1, pairs), 1)))
            else:
                edges.append((device(g, c, 1), device(g, path_at(g, 0, pairs), 0)))
    return edges


def exit_pairs(step, sections, pairs):
    edges = []

    def device(g, c, core):
        return g * pairs * 2 + c * 2 + core

    for g in range(sections):
        for place in range(pairs):
            c = path_at(g, place, pairs)
            if place < pairs - 1:
                edges.append((device(g, c, 0), device(g, c ^ step, 0)))
            elif g + 1 < sections:
                there = path_at(g + 1, pairs - 1, pairs) ^ step
                edges.append((device(g, c, 0), device(g + 1, there, 0)))
            if place > 0:
                edges.append((device(g, c, 1), device(g, c ^ step, 1)))
            elif g > 0:
                edges.append((device(g, c, 1), device(g - 1, path_at(g - 1, 0, pairs) ^ step, 1)))
    return edges


def shift_pairs(sections, pairs):
    where = [
        g * pairs * 2 + path_at(g, l, pairs) * 2 for g in range(sections) for l in range(pairs)
    ]
    up = [(where[z], where[z + 1]) for z in range(len(where) - 1)]
    down = [(where[z] + 1, where[z - 1] + 1) for z in range(1, len(where))]
    return up + down


def transform_tables(count):
    index = np.arange(count)
    angle = (index[:, None] * index[None, :] % count) * (2.0 * math.pi / count)
    parts = []
    for table in (np.cos(angle), np.sin(angle)):
        high = table.astype(np.float32).astype(jnp.bfloat16)
        parts += [high, (table - high.astype(np.float64)).astype(np.float32).astype(jnp.bfloat16)]
    return parts


def halves(value):
    high = value.astype(jnp.bfloat16)
    low = (value - high.astype(jnp.float32)).astype(jnp.bfloat16)
    return high, low


def cos_sin(angle):
    square = angle * angle
    sine = 1.0
    for n in (13, 11, 9, 7, 5, 3):
        scale = -1.0 / (n * (n - 1))
        sine = 1.0 + square * (scale * sine)
    cosine = 1.0
    for n in (14, 12, 10, 8, 6, 4, 2):
        scale = -1.0 / (n * (n - 1))
        cosine = 1.0 + square * (scale * cosine)
    return cosine, angle * sine


def multiplier(ref, rows, columns):
    def wave(count, axis):
        index = lax.broadcasted_iota(jnp.int32, (rows, columns), axis)
        folded = jnp.where(index < count // 2, index, index - count)
        return folded.astype(jnp.float32) * (2.0 * math.pi / count)

    wave_x, wave_y = wave(rows, 0), wave(columns, 1)
    argument = (OMEGA * ref) ** 2 - (wave_x * wave_x + wave_y * wave_y)
    vertical = jnp.sqrt(jnp.maximum(argument, 0.0)) * DEPTH_STEP
    evanescent = jnp.sqrt(jnp.maximum(-argument, 0.0)) * DEPTH_STEP
    factor = jnp.exp(-evanescent) * (1.0 / (rows * columns))
    cosine, sine = cos_sin(0.5 * vertical)
    return factor * (1.0 - 2.0 * sine * sine), factor * (-2.0 * sine * cosine)


def propagate(real, imag, mult_real, mult_imag, theta, x_tables, y_tables):
    rows, columns = real.shape

    def along_y(a, b, inverse):
        cos_high, cos_low, sin_high, sin_low = y_tables
        table = jnp.concatenate([cos_high, cos_high, cos_low, sin_high, sin_high, sin_low], axis=0)
        a_high, a_low = halves(a)
        b_high, b_low = halves(b)
        if inverse:
            top = [a_high, a_low, a_high, -b_high, -b_low, -b_high]
            bottom = [b_high, b_low, b_high, a_high, a_low, a_high]
        else:
            top = [a_high, a_low, a_high, b_high, b_low, b_high]
            bottom = [b_high, b_low, b_high, -a_high, -a_low, -a_high]
        out_real = jnp.dot(
            jnp.concatenate(top, axis=1), table, preferred_element_type=jnp.float32
        )
        out_imag = jnp.dot(
            jnp.concatenate(bottom, axis=1), table, preferred_element_type=jnp.float32
        )
        return out_real, out_imag

    def along_x(a, b, inverse):
        cos_high, cos_low, sin_high, sin_low = x_tables
        table = jnp.concatenate([cos_high, cos_high, cos_low, sin_high, sin_high, sin_low], axis=1)
        a_high, a_low = halves(a)
        b_high, b_low = halves(b)
        if inverse:
            left = [a_high, a_low, a_high, -b_high, -b_low, -b_high]
            right = [b_high, b_low, b_high, a_high, a_low, a_high]
        else:
            left = [a_high, a_low, a_high, b_high, b_low, b_high]
            right = [b_high, b_low, b_high, -a_high, -a_low, -a_high]
        out_real = jnp.dot(
            table, jnp.concatenate(left, axis=0), preferred_element_type=jnp.float32
        )
        out_imag = jnp.dot(
            table, jnp.concatenate(right, axis=0), preferred_element_type=jnp.float32
        )
        return out_real, out_imag

    real, imag = along_y(real, imag, False)
    real, imag = along_x(real, imag, False)
    real, imag = real * mult_real - imag * mult_imag, real * mult_imag + imag * mult_real
    real, imag = along_x(real, imag, True)
    real, imag = along_y(real, imag, True)
    cosine, sine = cos_sin(theta)
    return real * cosine + imag * sine, imag * cosine - real * sine


class Place:
    def __init__(self, pairs):
        index = lax.axis_index("lat")
        self.section = lax.axis_index("depth")
        self.pair = index // 2
        self.core = index % 2
        self.level = place_on(self.section, self.pair, pairs)
        self.first = self.level == 0
        self.last = self.level == pairs - 1
        self.pairs = pairs


def vmem_call(body, name, out_shapes, spaces, scratch=(), limit=24 << 20):
    memory = {"v": pltpu.VMEM, "s": pltpu.SMEM}
    return pl.pallas_call(
        body,
        name=name,
        out_shape=[jax.ShapeDtypeStruct(shape, jnp.float32) for shape in out_shapes],
        in_specs=[pl.BlockSpec(memory_space=memory[space]) for space in spaces],
        out_specs=[pl.BlockSpec(memory_space=pltpu.VMEM) for _ in out_shapes],
        scratch_shapes=list(scratch),
        compiler_params=pltpu.CompilerParams(vmem_limit_bytes=limit),
    )


def plane_shards(
    down_real,
    down_imaginary,
    up_real,
    up_imaginary,
    slowness,
    ref_slow,
    reflectivity,
    source_real,
    source_imaginary,
):
    levels, block, columns = down_real.shape
    sections = lax.axis_size("depth")
    lat_count = lax.axis_size("lat")
    pairs = lat_count // 2
    rows = block * lat_count
    both = 2 * block
    stack = levels * block
    fences = pairs // 2
    swap = [(index, index ^ 1) for index in range(lat_count)]
    x_tables = transform_tables(rows)
    y_tables = transform_tables(columns)
    f32 = jnp.float32

    def split_body(dr, di, ur, ui, slow, refl, sr, si, send, keep, *static):
        here = Place(pairs)

        def fill(out, real, imag):
            for n in range(levels):
                out[pl.ds(n * block, block), :] = real[n]
                out[pl.ds(stack + n * block, block), :] = imag[n]
                out[pl.ds(2 * stack + n * block, block), :] = slow[n]
            out[pl.ds(3 * stack, block), :] = sr[...]
            out[pl.ds(3 * stack + block, block), :] = si[...]

        @pl.when(here.core == 0)
        def _():
            fill(send, ur, ui)
            fill(keep, dr, di)

        @pl.when(here.core == 1)
        def _():
            fill(send, dr, di)
            fill(keep, ur, ui)

        for step in range(pairs):
            level = place_on(here.section, here.pair ^ step, pairs)
            static[step][pl.ds(0, block), :] = slow[level]
            static[step][pl.ds(block, block), :] = refl[level]

    long = 3 * stack + both
    outs = vmem_call(
        split_body,
        "split",
        [(long, columns)] * 2 + [(both, columns)] * pairs,
        "v" * 8,
    )(
        down_real,
        down_imaginary,
        up_real,
        up_imaginary,
        slowness,
        reflectivity,
        source_real,
        source_imaginary,
    )
    send, keep, static = outs[0], outs[1], outs[2:]
    got = lax.ppermute(send, "lat", swap)

    message = 3 * both + 8

    def gather_body(keep, got, ref, *messages):
        here = Place(pairs)
        mine = pl.multiple_of(here.core * block, block)
        other = pl.multiple_of((1 - here.core) * block, block)
        for step in range(pairs):
            place = place_on(here.section, here.pair ^ step, pairs)
            level = jnp.where(here.core == 0, place + levels - 1, place + 1) % levels
            start = pl.multiple_of(level * block, block)
            out = messages[step]
            value = ref[level]
            for part in range(3):
                less = value if part == 2 else 0.0
                take = pl.ds(pl.multiple_of(part * stack + start, block), block)
                out[pl.ds(part * both + mine, block), :] = keep[take, :] - less
                out[pl.ds(part * both + other, block), :] = got[take, :] - less
            out[pl.ds(3 * both, 8), :] = jnp.full((8, columns), value, f32)

            @pl.when((here.core == 1) & (here.section == 0) & (place == pairs - 1))
            def _():
                for part in range(2):
                    take = pl.ds(3 * stack + part * block, block)
                    out[pl.ds(part * both + mine, block), :] = keep[take, :]
                    out[pl.ds(part * both + other, block), :] = got[take, :]

    messages = vmem_call(
        gather_body, "gather", [(message, columns)] * pairs, "vvs"
    )(keep, got, ref_slow)
    arrived = [
        lax.ppermute(messages[step], ("depth", "lat"), entry_pairs(step, sections, pairs))
        for step in range(pairs)
    ]
    media = [static[0]] + [
        lax.ppermute(
            static[step], "lat", [(index, index ^ (2 * step)) for index in range(lat_count)]
        )
        for step in range(1, pairs)
    ]
    media_own = jnp.concatenate(media, axis=0)
    media_other = lax.ppermute(media_own, "lat", swap)

    tables_in = [jnp.asarray(t) for t in x_tables + y_tables]
    plane = (2 * rows, columns)
    scratch = [pltpu.VMEM((rows, columns), f32) for _ in range(4)]

    def first_body(*refs):
        pieces, tabs, out = refs[:pairs], refs[pairs : pairs + 8], refs[pairs + 8]
        real, imag, theta = refs[pairs + 9 : pairs + 12]
        here = Place(pairs)
        edge = ((here.core == 0) & here.first) | ((here.core == 1) & here.last)
        fence = jnp.where(edge, fences, 0)
        for step in range(pairs):
            start = pl.multiple_of((here.pair ^ step ^ fence) * both, both)
            real[pl.ds(start, both), :] = pieces[step][pl.ds(0, both), :]
            imag[pl.ds(start, both), :] = pieces[step][pl.ds(both, both), :]
            theta[pl.ds(start, both), :] = pieces[step][pl.ds(2 * both, both), :]
        top = (here.core == 0) & here.first & (here.section == 0)

        @pl.when(top)
        def _():
            out[pl.ds(0, rows), :] = real[...]
            out[pl.ds(rows, rows), :] = imag[...]

        @pl.when(jnp.logical_not(top))
        def _():
            ref = pieces[0][3 * both, 0]
            mult_real, mult_imag = multiplier(ref, rows, columns)
            new_real, new_imag = propagate(
                real[...],
                imag[...],
                mult_real,
                mult_imag,
                theta[...] * (OMEGA * DEPTH_STEP),
                [t[...] for t in tabs[:4]],
                [t[...] for t in tabs[4:]],
            )
            out[pl.ds(0, rows), :] = new_real
            out[pl.ds(rows, rows), :] = new_imag

    own0 = vmem_call(first_body, "tick0", [plane], "v" * (pairs + 8), scratch[:3])(
        *arrived, *tables_in
    )[0]
    other0 = lax.ppermute(own0, "lat", swap)

    def mixed(own, other, media_own, media_other, theta, refl, here, ref):
        for step in range(pairs):
            start = (here.pair ^ step) * both
            for piece, core in ((media_own, here.core), (media_other, 1 - here.core)):
                at = pl.multiple_of(start + core * block, block)
                theta[pl.ds(at, block), :] = (
                    piece[pl.ds(step * both, block), :] - ref
                ) * (OMEGA * DEPTH_STEP)
                refl[pl.ds(at, block), :] = piece[pl.ds(step * both + block, block), :]
        weight = refl[...] * jnp.where(here.core == 0, -1.0, 1.0)
        real = own[:rows] + weight * other[:rows]
        imag = own[rows:] + weight * other[rows:]
        return real, imag

    def middle_body(own, other, media_own, media_other, ref_slow, *refs):
        tabs, out, theta, refl = refs[:8], refs[8], refs[9], refs[10]
        here = Place(pairs)
        ref = ref_slow[here.level]
        real, imag = mixed(
            own[...], other[...], media_own, media_other, theta, refl, here, ref
        )
        mult_real, mult_imag = multiplier(ref, rows, columns)
        new_real, new_imag = propagate(
            real,
            imag,
            mult_real,
            mult_imag,
            theta[...],
            [t[...] for t in tabs[:4]],
            [t[...] for t in tabs[4:]],
        )
        out[pl.ds(0, rows), :] = new_real
        out[pl.ds(rows, rows), :] = new_imag

    moved = vmem_call(middle_body, "tick1", [plane], "vvvvs" + "v" * 8, scratch[:2])(
        own0, other0, media_own, media_other, ref_slow, *tables_in
    )[0]
    own1 = lax.ppermute(moved, ("depth", "lat"), shift_pairs(sections, pairs))
    other1 = lax.ppermute(own1, "lat", swap)

    def last_body(own, other, own0, other0, media_own, media_other, ref_slow, *refs):
        tabs, outs = refs[:8], refs[8 : 8 + pairs]
        theta, refl, real_s, imag_s = refs[8 + pairs :]
        here = Place(pairs)
        ref = ref_slow[here.level]
        top = here.first & (here.section == 0)

        own_kept = jnp.where(top & (here.core == 0), own0[...], own[...])
        other_kept = jnp.where(top & (here.core == 1), other0[...], other[...])
        real, imag = mixed(own_kept, other_kept, media_own, media_other, theta, refl, here, ref)
        mult_real, mult_imag = multiplier(ref, rows, columns)
        new_real, new_imag = propagate(
            real,
            imag,
            mult_real,
            mult_imag,
            theta[...],
            [t[...] for t in tabs[:4]],
            [t[...] for t in tabs[4:]],
        )
        real_s[...] = new_real
        imag_s[...] = new_imag
        edge = ((here.core == 0) & here.last) | ((here.core == 1) & here.first)
        fence = jnp.where(edge, fences, 0)
        for step in range(pairs):
            start = (here.pair ^ step ^ fence) * both
            for n, core in enumerate((here.core, 1 - here.core)):
                take = pl.ds(pl.multiple_of(start + core * block, block), block)
                outs[step][pl.ds(n * both, block), :] = real_s[take, :]
                outs[step][pl.ds(n * both + block, block), :] = imag_s[take, :]

    leaving = vmem_call(
        last_body, "tick2", [(2 * both, columns)] * pairs, "vvvvvvs" + "v" * 8, scratch
    )(own1, other1, own0, other0, media_own, media_other, ref_slow, *tables_in)
    back = [
        lax.ppermute(leaving[step], ("depth", "lat"), exit_pairs(step, sections, pairs))
        for step in range(pairs)
    ]
    crossed = [lax.ppermute(piece[both:], "lat", swap) for piece in back]

    def mix_body(*refs):
        own, other = refs[:pairs], refs[pairs : 2 * pairs]
        refl, sr, si = refs[2 * pairs : 2 * pairs + 3]
        dr, di, ur, ui = refs[2 * pairs + 3 : 2 * pairs + 7]
        down, up = refs[2 * pairs + 7 :]
        here = Place(pairs)

        def place_pieces(down_pieces, up_pieces):
            for step in range(pairs):
                place = place_on(here.section, here.pair ^ step, pairs)
                down[(place + 1) % levels] = down_pieces[step][pl.ds(0, both), :]
                up[(place + levels - 1) % levels] = up_pieces[step][pl.ds(0, both), :]

        @pl.when(here.core == 0)
        def _():
            place_pieces(own, other)

        @pl.when(here.core == 1)
        def _():
            place_pieces(other, own)

        @pl.when(here.section == 0)
        def _():
            down[0, pl.ds(0, block), :] = sr[...]
            down[0, pl.ds(block, block), :] = si[...]

        for n in range(levels):
            r = refl[n]
            d_real, d_imag = down[n, pl.ds(0, block), :], down[n, pl.ds(block, block), :]
            u_real, u_imag = up[n, pl.ds(0, block), :], up[n, pl.ds(block, block), :]
            dr[n] = d_real - r * u_real
            di[n] = d_imag - r * u_imag
            ur[n] = u_real + r * d_real
            ui[n] = u_imag + r * d_imag

    return tuple(
        vmem_call(
            mix_body,
            "mix",
            [(levels, block, columns)] * 4,
            "v" * (2 * pairs + 3),
            [pltpu.VMEM((levels, both, columns), f32) for _ in range(2)],
        )(*back, *crossed, reflectivity, source_real, source_imaginary)
    )


def shards(*arrays):
    levels, block, columns = arrays[0].shape
    pairs = lax.axis_size("lat") // 2
    fits = (
        lax.axis_size("lat") == 2 * levels
        and levels >= 2
        and levels & (levels - 1) == 0
        and block % 8 == 0
        and columns % 128 == 0
        and TICKS == 3
    )
    return plane_shards(*arrays) if fits else row_shards(*arrays)


def solution(mesh):
    placed = (
        P("depth", "lat", None),
        P("depth", "lat", None),
        P("depth", "lat", None),
        P("depth", "lat", None),
        P("depth", "lat", None),
        P("depth"),
        P("depth", "lat", None),
        P("lat", None),
        P("lat", None),
    )
    return jax.shard_map(
        shards,
        mesh=mesh,
        in_specs=placed,
        out_specs=(
            P("depth", "lat", None),
            P("depth", "lat", None),
            P("depth", "lat", None),
            P("depth", "lat", None),
        ),
        check_vma=False,
    )
```

```python
import math

import jax
import jax.numpy as jnp
import numpy as np
from jax import lax
from jax.experimental import pallas as pl
from jax.experimental.pallas import tpu as pltpu
from jax.sharding import PartitionSpec as P


TICKS = 3

OMEGA = 2.5
DEPTH_STEP = 1.0


def passed_along(value, axis, steps):
    count = lax.axis_size(axis)
    initial, last = (max(0, -steps), min(count, count - steps))
    return lax.ppermute(value, axis, [(source, source + steps) for source in range(initial, last)])


def tables(count):
    index = jnp.arange(count, dtype=jnp.int32)
    phase = index[:, None] * index[None, :] % count
    angle = phase.astype(jnp.float32) * (2.0 * math.pi / count)
    return (jnp.cos(angle), jnp.sin(angle))


def wrapped_numbers(index, count):
    folded = jnp.where(index < count // 2, index, index - count)
    return folded.astype(jnp.float32) * (2.0 * math.pi / count)


def complex_product(form, real, imag, cosine, sine, inverse):
    real_cos = jnp.einsum(form, real, cosine, precision=lax.Precision.HIGHEST)
    real_sin = jnp.einsum(form, real, sine, precision=lax.Precision.HIGHEST)
    imag_cos = jnp.einsum(form, imag, cosine, precision=lax.Precision.HIGHEST)
    imag_sin = jnp.einsum(form, imag, sine, precision=lax.Precision.HIGHEST)
    if inverse:
        return (real_cos - imag_sin, imag_cos + real_sin)
    return (real_cos + imag_sin, imag_cos - real_sin)


def spectral(real, imag, mult_real, mult_imag, corr_real, corr_imag, all_tables, lat_count):
    cos_y, sin_y, cos_x, sin_x = all_tables
    planes = real.shape[0]
    rows_here = real.shape[1]
    width_y = real.shape[2]
    width_x = rows_here * lat_count
    cols_here = width_y // lat_count
    first_real, first_imag = complex_product("nxy,yk->xkn", real, imag, cos_y, sin_y, False)
    send_real = jnp.swapaxes(
        first_real.reshape(rows_here, lat_count, cols_here, planes), 0, 1
    ).reshape(lat_count, rows_here * cols_here * planes)
    send_imag = jnp.swapaxes(
        first_imag.reshape(rows_here, lat_count, cols_here, planes), 0, 1
    ).reshape(lat_count, rows_here * cols_here * planes)
    got_real, got_imag = (
        lax.all_to_all(send_real, "lat", split_axis=0, concat_axis=0, tiled=True),
        lax.all_to_all(send_imag, "lat", split_axis=0, concat_axis=0, tiled=True),
    )
    got_real = got_real.reshape(width_x, cols_here, planes)
    got_imag = got_imag.reshape(width_x, cols_here, planes)
    spec_real, spec_imag = complex_product("xqn,xp->nqp", got_real, got_imag, cos_x, sin_x, False)
    moved_real = spec_real * mult_real - spec_imag * mult_imag
    moved_imag = spec_real * mult_imag + spec_imag * mult_real
    back_real, back_imag = complex_product(
        "nqp,px->qxn", moved_real, moved_imag, cos_x, sin_x, True
    )
    back_real = jnp.swapaxes(
        (back_real / width_x).reshape(cols_here, lat_count, rows_here, planes), 0, 1
    ).reshape(lat_count, cols_here * rows_here * planes)
    back_imag = jnp.swapaxes(
        (back_imag / width_x).reshape(cols_here, lat_count, rows_here, planes), 0, 1
    ).reshape(lat_count, cols_here * rows_here * planes)
    ret_real, ret_imag = (
        lax.all_to_all(back_real, "lat", split_axis=0, concat_axis=0, tiled=True),
        lax.all_to_all(back_imag, "lat", split_axis=0, concat_axis=0, tiled=True),
    )
    ret_real = ret_real.reshape(width_y, rows_here, planes)
    ret_imag = ret_imag.reshape(width_y, rows_here, planes)
    plane_real, plane_imag = complex_product("kxn,ky->nxy", ret_real, ret_imag, cos_y, sin_y, True)
    plane_real = plane_real / width_y
    plane_imag = plane_imag / width_y
    final_real = plane_real * corr_real - plane_imag * corr_imag
    final_imag = plane_real * corr_imag + plane_imag * corr_real
    return (final_real, final_imag)


def media_factors(slow_planes, slow_refs, lat_count, lat_index):
    rows_here = slow_planes.shape[1]
    width_y = slow_planes.shape[2]
    width_x = rows_here * lat_count
    cols_here = width_y // lat_count
    wave_x = wrapped_numbers(jnp.arange(width_x, dtype=jnp.int32), width_x)
    wave_y = wrapped_numbers(
        lat_index * cols_here + jnp.arange(cols_here, dtype=jnp.int32), width_y
    )
    squared = wave_y[:, None] ** 2 + wave_x[None, :] ** 2
    argument = (OMEGA * slow_refs[:, None, None]) ** 2 - squared[None]
    vertical = jnp.sqrt(jnp.maximum(argument, 0.0)) * DEPTH_STEP
    evanescent = jnp.sqrt(jnp.maximum(-argument, 0.0)) * DEPTH_STEP
    factor = jnp.exp(-evanescent)
    theta = OMEGA * (slow_planes - slow_refs[:, None, None]) * DEPTH_STEP
    return (
        factor * jnp.cos(vertical),
        -factor * jnp.sin(vertical),
        jnp.cos(theta),
        -jnp.sin(theta),
    )


def row_shards(
    down_real,
    down_imaginary,
    up_real,
    up_imaginary,
    slowness,
    ref_slow,
    reflectivity,
    source_real,
    source_imaginary,
):
    levels = down_real.shape[0]
    lat_count = lax.axis_size("lat")
    lat_index = lax.axis_index("lat")
    top_mask = (lax.axis_index("depth") == 0).astype(jnp.float32)
    width_x = down_real.shape[1] * lat_count
    cos_y, sin_y = tables(down_real.shape[2])
    cos_x, sin_x = tables(width_x)
    all_tables = (cos_y, sin_y, cos_x, sin_x)
    slow_planes = jnp.concatenate([slowness, slowness], axis=0)
    slow_refs = jnp.concatenate([ref_slow, ref_slow], axis=0)
    mult_real, mult_imag, corr_real, corr_imag = media_factors(
        slow_planes, slow_refs, lat_count, lat_index
    )
    for _ in range(TICKS):
        joined_real = jnp.concatenate([down_real, up_real], axis=0)
        joined_imag = jnp.concatenate([down_imaginary, up_imaginary], axis=0)
        prop_real, prop_imag = spectral(
            joined_real,
            joined_imag,
            mult_real,
            mult_imag,
            corr_real,
            corr_imag,
            all_tables,
            lat_count,
        )
        above_real, above_imag = passed_along(
            (prop_real[levels - 1], prop_imag[levels - 1]), "depth", 1
        )
        below_real, below_imag = passed_along((prop_real[levels], prop_imag[levels]), "depth", -1)
        head_real = above_real + top_mask * source_real
        head_imag = above_imag + top_mask * source_imaginary
        in_down_real = jnp.concatenate([head_real[None], prop_real[: levels - 1]], axis=0)
        in_down_imag = jnp.concatenate([head_imag[None], prop_imag[: levels - 1]], axis=0)
        in_up_real = jnp.concatenate([prop_real[levels + 1 :], below_real[None]], axis=0)
        in_up_imag = jnp.concatenate([prop_imag[levels + 1 :], below_imag[None]], axis=0)
        down_real = in_down_real - reflectivity * in_up_real
        down_imaginary = in_down_imag - reflectivity * in_up_imag
        up_real = in_up_real + reflectivity * in_down_real
        up_imaginary = in_up_imag + reflectivity * in_down_imag
    return (down_real, down_imaginary, up_real, up_imaginary)


def path_at(section, place, pairs):
    place = place if section % 2 == 0 else pairs - 1 - place
    return place ^ (place >> 1)


def place_on(section, pair, pairs):
    shift, place = 1, pair
    while (1 << shift) <= pairs:
        place = place ^ (pair >> shift)
        shift += 1
    return jnp.where(section % 2 == 0, place, pairs - 1 - place)


def level_pairs(sections, pairs, parity):
    where = [
        g * pairs * 2 + path_at(g, l, pairs) * 2 for g in range(sections) for l in range(pairs)
    ]
    edges = []
    for z in range(parity, len(where) - 1, 2):
        for core in range(2):
            here, below = where[z] + core, where[z + 1] + core
            edges += [(here, below), (below, here)]
    return edges


def section_pairs(sections, pairs, parity):
    width = 2 * pairs
    edges = []
    for g in range(parity, sections - 1, 2):
        for n in range(width):
            edges += [(g * width + n, (g + 1) * width + n), ((g + 1) * width + n, g * width + n)]
    return edges


def transform_tables(count, order, transposed):
    index = np.arange(count)
    angle = (index[:, None] * np.asarray(order)[None, :] % count) * (2.0 * math.pi / count)
    if transposed:
        angle = angle.T
    parts = []
    for table in (np.cos(angle), np.sin(angle)):
        high = table.astype(np.float32).astype(jnp.bfloat16)
        parts += [high, (table - high.astype(np.float64)).astype(np.float32).astype(jnp.bfloat16)]
    return parts


def halves(value):
    high = value.astype(jnp.bfloat16)
    low = (value - high.astype(jnp.float32)).astype(jnp.bfloat16)
    return high, low


def cos_sin(angle):
    square = angle * angle
    sine = 1.0
    for n in (13, 11, 9, 7, 5, 3):
        scale = -1.0 / (n * (n - 1))
        sine = 1.0 + square * (scale * sine)
    cosine = 1.0
    for n in (14, 12, 10, 8, 6, 4, 2):
        scale = -1.0 / (n * (n - 1))
        cosine = 1.0 + square * (scale * cosine)
    return cosine, angle * sine


def multiplier(ref, rows, columns, first, here_columns):
    def wave(count, axis, start):
        index = lax.broadcasted_iota(jnp.int32, (rows, here_columns), axis) + start
        folded = jnp.where(index < count // 2, index, index - count)
        return folded.astype(jnp.float32) * (2.0 * math.pi / count)

    wave_x, wave_y = wave(rows, 0, 0), wave(columns, 1, first)
    argument = (OMEGA * ref) ** 2 - (wave_x * wave_x + wave_y * wave_y)
    vertical = jnp.sqrt(jnp.maximum(argument, 0.0)) * DEPTH_STEP
    evanescent = jnp.sqrt(jnp.maximum(-argument, 0.0)) * DEPTH_STEP
    factor = jnp.exp(-evanescent) * (1.0 / (rows * columns))
    cosine, sine = cos_sin(0.5 * vertical)
    return factor * (1.0 - 2.0 * sine * sine), factor * (-2.0 * sine * cosine)


def terms(a, b, inverse):
    a_high, a_low = halves(a)
    b_high, b_low = halves(b)
    if inverse:
        real = [a_high, a_low, a_high, -b_high, -b_low, -b_high]
        imag = [b_high, b_low, b_high, a_high, a_low, a_high]
    else:
        real = [a_high, a_low, a_high, b_high, b_low, b_high]
        imag = [b_high, b_low, b_high, -a_high, -a_low, -a_high]
    return real, imag


def table_of(parts, axis):
    cos_high, cos_low, sin_high, sin_low = (part[...] for part in parts)
    return jnp.concatenate(
        [cos_high, cos_high, cos_low, sin_high, sin_high, sin_low], axis=axis
    )


def along_y(a, b, parts, inverse):
    count = a.shape[0]
    real, imag = (jnp.concatenate(t, axis=1) for t in terms(a, b, inverse))
    out = jnp.dot(
        jnp.concatenate([real, imag], axis=0),
        table_of(parts, 0),
        preferred_element_type=jnp.float32,
    )
    return out[:count], out[count:]


def along_x(a, b, parts, inverse):
    count = a.shape[1]
    real, imag = (jnp.concatenate(t, axis=0) for t in terms(a, b, inverse))
    out = jnp.dot(
        table_of(parts, 1),
        jnp.concatenate([real, imag], axis=1),
        preferred_element_type=jnp.float32,
    )
    return out[:, :count], out[:, count:]


class Place:
    def __init__(self, pairs):
        index = lax.axis_index("lat")
        self.section = lax.axis_index("depth")
        self.pair = index // 2
        self.core = index % 2
        self.level = place_on(self.section, self.pair, pairs)
        self.first = self.level == 0
        self.last = self.level == pairs - 1


def local_call(body, out_shapes, spaces, scratch=(), limit=24 << 20):
    memory = {"v": pltpu.VMEM, "s": pltpu.SMEM, "h": pltpu.HBM}
    return pl.pallas_call(
        body,
        out_shape=[jax.ShapeDtypeStruct(shape, jnp.float32) for shape in out_shapes],
        in_specs=[pl.BlockSpec(memory_space=memory[space]) for space in spaces],
        out_specs=[pl.BlockSpec(memory_space=pltpu.VMEM) for _ in out_shapes],
        scratch_shapes=list(scratch),
        compiler_params=pltpu.CompilerParams(vmem_limit_bytes=limit),
    )


def plane_shards(
    down_real,
    down_imaginary,
    up_real,
    up_imaginary,
    slowness,
    ref_slow,
    reflectivity,
    source_real,
    source_imaginary,
):
    levels, block, columns = down_real.shape
    sections = lax.axis_size("depth")
    lat_count = lax.axis_size("lat")
    pairs = lat_count // 2
    rows = block * lat_count
    tall = rows // 2
    wide = columns // 2
    two, four = 2 * block, 4 * block
    swap = [(index, index ^ 1) for index in range(lat_count)]
    place = np.arange(rows)
    order = place % tall // block * two + place // tall * block + place % block
    y_tables = [jnp.asarray(t) for t in transform_tables(columns, np.arange(columns), False)]
    x_tables = [jnp.asarray(t) for t in transform_tables(rows, order, False)]
    back_tables = [jnp.asarray(t) for t in transform_tables(rows, order, True)]
    f32 = jnp.float32
    local = (2 * tall, columns)
    part = (2 * tall, wide)

    def across(step):
        return [(index, index ^ (2 * step)) for index in range(lat_count)]

    def top(here):
        return here.first & (here.section == 0)

    def split_body(dr, di, ur, ui, slow, refl, sr, si, *rest):
        planes, media, sems = rest[:pairs], rest[pairs : 2 * pairs], rest[2 * pairs]
        here = Place(pairs)

        def pieces(step, first, second):
            level = place_on(here.section, here.pair ^ step, pairs)
            out = []
            for n, array in enumerate(first + second):
                source = array if len(array.shape) == 2 else array.at[level]
                out.append((source, planes[step].at[pl.ds(n * block, block), :]))
            out.append((slow.at[level], media[step].at[pl.ds(0, block), :]))
            out.append((refl.at[level], media[step].at[pl.ds(block, block), :]))
            return [
                pltpu.make_async_copy(source, target, sems.at[step * 6 + n])
                for n, (source, target) in enumerate(out)
            ]

        def each(act):
            for step in range(pairs):
                level = place_on(here.section, here.pair ^ step, pairs)
                sourced = (level == 0) & (here.section == 0)

                @pl.when(sourced)
                def _():
                    for move in pieces(step, (dr, di), (sr, si)):
                        act(move)

                @pl.when((level % 2 == 0) & jnp.logical_not(sourced))
                def _():
                    for move in pieces(step, (dr, di), (ur, ui)):
                        act(move)

                @pl.when(level % 2 == 1)
                def _():
                    for move in pieces(step, (ur, ui), (dr, di)):
                        act(move)

        each(lambda move: move.start())
        each(lambda move: move.wait())

    outs = local_call(
        split_body,
        [(four, columns)] * pairs + [(two, columns)] * pairs,
        "h" * 8,
        [pltpu.SemaphoreType.DMA((6 * pairs,))],
    )(
        *(
            pltpu.with_memory_space_constraint(array, pltpu.HBM)
            for array in (
                down_real,
                down_imaginary,
                up_real,
                up_imaginary,
                slowness,
                reflectivity,
                source_real,
                source_imaginary,
            )
        )
    )

    def exchanged(pieces):
        moved = [pieces[0]]
        for step in range(1, pairs):
            moved.append(lax.ppermute(pieces[step], "lat", across(step)))
        return moved

    planes = exchanged(outs[:pairs])
    media = exchanged(outs[pairs:])

    def multiplier_body(ref_slow, out):
        here = Place(pairs)
        real, imag = multiplier(ref_slow[here.level], rows, columns, here.core * wide, wide)
        out[:rows] = real
        out[rows:] = imag

    mult = local_call(multiplier_body, [(2 * rows, wide)], "s")(ref_slow)[0]

    def media_body(*refs):
        pieces, ref_slow, corr, refl = refs[:pairs], refs[pairs], refs[pairs + 1], refs[pairs + 2]
        here = Place(pairs)
        ref = ref_slow[here.level]
        for step in range(pairs):
            start = (here.pair ^ step) * block
            theta = (pieces[step][pl.ds(0, block), :] - ref) * (OMEGA * DEPTH_STEP)
            cosine, sine = cos_sin(theta)
            corr[pl.ds(pl.multiple_of(start, block), block), :] = cosine
            corr[pl.ds(pl.multiple_of(tall + start, block), block), :] = sine
            refl[pl.ds(pl.multiple_of(start, block), block), :] = pieces[step][
                pl.ds(block, block), :
            ]

    corr, refl = local_call(media_body, [local, (tall, columns)], "v" * pairs + "s")(
        *media, ref_slow
    )

    def halved(real, imag, here, axis, keep, send):
        def put(mine, theirs):
            keep[:tall], keep[tall:] = mine
            send[:tall], send[tall:] = theirs

        if axis == 0:
            cuts = [(real[:tall], imag[:tall]), (real[tall:], imag[tall:])]
        else:
            cuts = [(real[:, :wide], imag[:, :wide]), (real[:, wide:], imag[:, wide:])]

        @pl.when(here.core == 0)
        def _():
            put(cuts[0], cuts[1])

        @pl.when(here.core == 1)
        def _():
            put(cuts[1], cuts[0])

    def enter(which):
        def body(*refs):
            pieces, tabs, keep, send = refs[:pairs], refs[pairs : pairs + 4], *refs[pairs + 4 : -1]
            whole = refs[-1]
            here = Place(pairs)
            for step in range(pairs):
                start = (here.pair ^ step) * block
                for n in range(2):
                    whole[pl.ds(pl.multiple_of(n * tall + start, block), block), :] = pieces[step][
                        pl.ds((2 * which + n) * block, block), :
                    ]
            halved(*along_y(whole[:tall], whole[tall:], tabs, False), here, 1, keep, send)

        return local_call(body, [part, part, local], "v" * (pairs + 4))(
            *planes, *y_tables
        )

    def mixed(which, ahead, behind, source):
        def body(ahead, behind, source, refl, *refs):
            tabs, keep, send = refs[:4], refs[4], refs[5]
            here = Place(pairs)
            sign = jnp.where((here.level % 2 == 0) == (which == 0), -1.0, 1.0)
            behind = jnp.where(top(here), source[...], behind[...])
            base, side = (behind, ahead[...]) if which == 0 else (ahead[...], behind)
            weight = refl[...] * sign
            real = base[:tall] + weight * side[:tall]
            imag = base[tall:] + weight * side[tall:]
            halved(*along_y(real, imag, tabs, False), here, 1, keep, send)

        return local_call(body, [part, part], "v" * 8)(ahead, behind, source, refl, *y_tables)

    def column(keep, got):
        def body(keep, got, mult, *refs):
            tabs, back, out, send, real, imag = refs[:4], refs[4:8], *refs[8:]
            here = Place(pairs)
            for piece, core in ((keep, here.core), (got, 1 - here.core)):
                take = pl.ds(pl.multiple_of(core * tall, tall), tall)
                real[take, :] = piece[:tall]
                imag[take, :] = piece[tall:]
            a, b = along_x(real[...], imag[...], tabs, False)
            mult_real, mult_imag = mult[:rows], mult[rows:]
            a, b = a * mult_real - b * mult_imag, a * mult_imag + b * mult_real
            halved(*along_x(a, b, back, True), here, 0, out, send)

        return local_call(
            body, [part, part], "v" * 11, [pltpu.VMEM((rows, wide), f32) for _ in range(2)]
        )(keep, got, mult, *x_tables, *back_tables)

    def corrected(keep, got, corr, tabs, here, whole):
        for piece, core in ((keep, here.core), (got, 1 - here.core)):
            whole[:, pl.ds(pl.multiple_of(core * wide, wide), wide)] = piece[...]
        real, imag = along_y(whole[:tall], whole[tall:], tabs, True)
        cosine, sine = corr[:tall], corr[tall:]
        return real * cosine + imag * sine, imag * cosine - real * sine

    def leave(keep, got, *held):
        def body(keep, got, corr, *refs):
            kept, tabs, outs = refs[: len(held)], refs[len(held) : len(held) + 4], refs[4 + len(held) :]
            whole = outs[-1]
            for source, target in zip(kept, outs[1:]):
                target[...] = source[...]
            real, imag = corrected(keep, got, corr, tabs, Place(pairs), whole)
            outs[0][:tall], outs[0][tall:] = real, imag

        return local_call(
            body, [local] * (1 + len(held)), "v" * (7 + len(held)), [pltpu.VMEM(local, f32)]
        )(keep, got, corr, *held, *y_tables)

    def leave_last(keep, got):
        def body(keep, got, corr, *refs):
            tabs, outs, whole = refs[:4], refs[4 : 4 + pairs], refs[4 + pairs]
            here = Place(pairs)
            real, imag = corrected(keep, got, corr, tabs, here, whole)
            whole[:tall], whole[tall:] = real, imag
            for step in range(pairs):
                start = (here.pair ^ step) * block
                for m in range(2):
                    outs[step][pl.ds(m * block, block), :] = whole[
                        pl.ds(pl.multiple_of(m * tall + start, block), block), :
                    ]

        return local_call(
            body, [(two, columns)] * pairs, "v" * 7, [pltpu.VMEM(local, f32)]
        )(keep, got, corr, *y_tables)

    def crossed(value):
        return lax.ppermute(value, "lat", swap)

    keep0, send0, _ = enter(0)
    got0 = crossed(send0)
    keep1, send1, source = enter(1)
    got1 = crossed(send1)
    for _ in range(TICKS - 1):
        keep0, send0 = column(keep0, got0)
        got0 = crossed(send0)
        keep1, send1 = column(keep1, got1)
        got1 = crossed(send1)
        first = leave(keep0, got0)[0]
        second, first = leave(keep1, got1, first)
        ahead = lax.ppermute(first, ("depth", "lat"), level_pairs(sections, pairs, 0))
        behind = lax.ppermute(second, ("depth", "lat"), level_pairs(sections, pairs, 1))
        keep1, send1 = mixed(1, ahead, behind, source)
        got1 = crossed(send1)
        keep0, send0 = mixed(0, ahead, behind, source)
        got0 = crossed(send0)
    keep1, send1 = column(keep1, got1)
    got1 = crossed(send1)
    keep0, send0 = column(keep0, got0)
    got0 = crossed(send0)
    back1 = exchanged(leave_last(keep1, got1))
    leaving = leave_last(keep0, got0)
    back0 = exchanged(leaving)

    def pick_body(*refs):
        pieces, even, odd = refs[:pairs], refs[pairs], refs[pairs + 1]
        here = Place(pairs)
        for step in range(pairs):
            level = place_on(here.section, here.pair ^ step, pairs)
            for edge, mine in ((pairs - 1, 0), (0, 1)):
                for target, parity in ((even, mine), (odd, 1 - mine)):

                    @pl.when((level == edge) & (here.section % 2 == parity))
                    def _():
                        target[...] = pieces[step][...]

    even, odd = local_call(pick_body, [(two, columns)] * 2, "v" * pairs)(*back1)
    even = lax.ppermute(even, ("depth", "lat"), section_pairs(sections, pairs, 0))
    odd = lax.ppermute(odd, ("depth", "lat"), section_pairs(sections, pairs, 1))

    def mix_body(*refs):
        first, second = refs[:pairs], refs[pairs : 2 * pairs]
        even, odd, refl, sr, si = refs[2 * pairs : 2 * pairs + 5]
        dr, di, ur, ui, down, up = refs[2 * pairs + 5 :]
        here = Place(pairs)
        for step in range(pairs):
            level = place_on(here.section, here.pair ^ step, pairs)
            below, above = (level + 1) % levels, (level + levels - 1) % levels

            @pl.when(level % 2 == 0)
            def _():
                down[below] = first[step][...]
                up[above] = second[step][...]

            @pl.when(level % 2 == 1)
            def _():
                down[below] = second[step][...]
                up[above] = first[step][...]

        @pl.when(here.section % 2 == 0)
        def _():
            down[0] = odd[...]
            up[levels - 1] = even[...]

        @pl.when(here.section % 2 == 1)
        def _():
            down[0] = even[...]
            up[levels - 1] = odd[...]

        @pl.when(here.section == 0)
        def _():
            down[0, pl.ds(0, block), :] = sr[...]
            down[0, pl.ds(block, block), :] = si[...]

        for n in range(levels):
            r = refl[n]
            d_real, d_imag = down[n, pl.ds(0, block), :], down[n, pl.ds(block, block), :]
            u_real, u_imag = up[n, pl.ds(0, block), :], up[n, pl.ds(block, block), :]
            dr[n] = d_real - r * u_real
            di[n] = d_imag - r * u_imag
            ur[n] = u_real + r * d_real
            ui[n] = u_imag + r * d_imag

    return tuple(
        local_call(
            mix_body,
            [(levels, block, columns)] * 4,
            "v" * (2 * pairs + 5),
            [pltpu.VMEM((levels, two, columns), f32) for _ in range(2)],
        )(*back0, *back1, even, odd, reflectivity, source_real, source_imaginary)
    )


def fits(shape, mesh):
    levels, rows, columns = shape
    levels = levels // mesh.shape["depth"]
    return (
        mesh.shape["lat"] == 2 * levels
        and levels >= 2
        and levels & (levels - 1) == 0
        and rows // mesh.shape["lat"] % 8 == 0
        and columns % 256 == 0
    )


def solution(mesh):
    rows = P("depth", "lat", None)
    placed = (rows,) * 5 + (P("depth"), rows, P("lat", None), P("lat", None))

    def mapped(body):
        return jax.shard_map(
            body, mesh=mesh, in_specs=placed, out_specs=(rows,) * 4, check_vma=False
        )

    by_planes = mapped(plane_shards)
    by_rows = mapped(row_shards)

    def run(*arrays):
        return (by_planes if fits(arrays[0].shape, mesh) else by_rows)(*arrays)

    return run
```

```python
import math

import jax
import jax.numpy as jnp
import numpy as np
from jax import lax
from jax.experimental import pallas as pl
from jax.experimental.pallas import tpu as pltpu
from jax.sharding import PartitionSpec as P


TICKS = 3

OMEGA = 2.5
DEPTH_STEP = 1.0


def passed_along(value, axis, steps):
    count = lax.axis_size(axis)
    initial, last = (max(0, -steps), min(count, count - steps))
    return lax.ppermute(value, axis, [(source, source + steps) for source in range(initial, last)])


def tables(count):
    index = jnp.arange(count, dtype=jnp.int32)
    phase = index[:, None] * index[None, :] % count
    angle = phase.astype(jnp.float32) * (2.0 * math.pi / count)
    return (jnp.cos(angle), jnp.sin(angle))


def wrapped_numbers(index, count):
    folded = jnp.where(index < count // 2, index, index - count)
    return folded.astype(jnp.float32) * (2.0 * math.pi / count)


def complex_product(form, real, imag, cosine, sine, inverse):
    real_cos = jnp.einsum(form, real, cosine, precision=lax.Precision.HIGHEST)
    real_sin = jnp.einsum(form, real, sine, precision=lax.Precision.HIGHEST)
    imag_cos = jnp.einsum(form, imag, cosine, precision=lax.Precision.HIGHEST)
    imag_sin = jnp.einsum(form, imag, sine, precision=lax.Precision.HIGHEST)
    if inverse:
        return (real_cos - imag_sin, imag_cos + real_sin)
    return (real_cos + imag_sin, imag_cos - real_sin)


def spectral(real, imag, mult_real, mult_imag, corr_real, corr_imag, all_tables, lat_count):
    cos_y, sin_y, cos_x, sin_x = all_tables
    planes = real.shape[0]
    rows_here = real.shape[1]
    width_y = real.shape[2]
    width_x = rows_here * lat_count
    cols_here = width_y // lat_count
    first_real, first_imag = complex_product("nxy,yk->xkn", real, imag, cos_y, sin_y, False)
    send_real = jnp.swapaxes(
        first_real.reshape(rows_here, lat_count, cols_here, planes), 0, 1
    ).reshape(lat_count, rows_here * cols_here * planes)
    send_imag = jnp.swapaxes(
        first_imag.reshape(rows_here, lat_count, cols_here, planes), 0, 1
    ).reshape(lat_count, rows_here * cols_here * planes)
    got_real, got_imag = (
        lax.all_to_all(send_real, "lat", split_axis=0, concat_axis=0, tiled=True),
        lax.all_to_all(send_imag, "lat", split_axis=0, concat_axis=0, tiled=True),
    )
    got_real = got_real.reshape(width_x, cols_here, planes)
    got_imag = got_imag.reshape(width_x, cols_here, planes)
    spec_real, spec_imag = complex_product("xqn,xp->nqp", got_real, got_imag, cos_x, sin_x, False)
    moved_real = spec_real * mult_real - spec_imag * mult_imag
    moved_imag = spec_real * mult_imag + spec_imag * mult_real
    back_real, back_imag = complex_product(
        "nqp,px->qxn", moved_real, moved_imag, cos_x, sin_x, True
    )
    back_real = jnp.swapaxes(
        (back_real / width_x).reshape(cols_here, lat_count, rows_here, planes), 0, 1
    ).reshape(lat_count, cols_here * rows_here * planes)
    back_imag = jnp.swapaxes(
        (back_imag / width_x).reshape(cols_here, lat_count, rows_here, planes), 0, 1
    ).reshape(lat_count, cols_here * rows_here * planes)
    ret_real, ret_imag = (
        lax.all_to_all(back_real, "lat", split_axis=0, concat_axis=0, tiled=True),
        lax.all_to_all(back_imag, "lat", split_axis=0, concat_axis=0, tiled=True),
    )
    ret_real = ret_real.reshape(width_y, rows_here, planes)
    ret_imag = ret_imag.reshape(width_y, rows_here, planes)
    plane_real, plane_imag = complex_product("kxn,ky->nxy", ret_real, ret_imag, cos_y, sin_y, True)
    plane_real = plane_real / width_y
    plane_imag = plane_imag / width_y
    final_real = plane_real * corr_real - plane_imag * corr_imag
    final_imag = plane_real * corr_imag + plane_imag * corr_real
    return (final_real, final_imag)


def media_factors(slow_planes, slow_refs, lat_count, lat_index):
    rows_here = slow_planes.shape[1]
    width_y = slow_planes.shape[2]
    width_x = rows_here * lat_count
    cols_here = width_y // lat_count
    wave_x = wrapped_numbers(jnp.arange(width_x, dtype=jnp.int32), width_x)
    wave_y = wrapped_numbers(
        lat_index * cols_here + jnp.arange(cols_here, dtype=jnp.int32), width_y
    )
    squared = wave_y[:, None] ** 2 + wave_x[None, :] ** 2
    argument = (OMEGA * slow_refs[:, None, None]) ** 2 - squared[None]
    vertical = jnp.sqrt(jnp.maximum(argument, 0.0)) * DEPTH_STEP
    evanescent = jnp.sqrt(jnp.maximum(-argument, 0.0)) * DEPTH_STEP
    factor = jnp.exp(-evanescent)
    theta = OMEGA * (slow_planes - slow_refs[:, None, None]) * DEPTH_STEP
    return (
        factor * jnp.cos(vertical),
        -factor * jnp.sin(vertical),
        jnp.cos(theta),
        -jnp.sin(theta),
    )


def row_shards(
    down_real,
    down_imaginary,
    up_real,
    up_imaginary,
    slowness,
    ref_slow,
    reflectivity,
    source_real,
    source_imaginary,
):
    levels = down_real.shape[0]
    lat_count = lax.axis_size("lat")
    lat_index = lax.axis_index("lat")
    top_mask = (lax.axis_index("depth") == 0).astype(jnp.float32)
    width_x = down_real.shape[1] * lat_count
    cos_y, sin_y = tables(down_real.shape[2])
    cos_x, sin_x = tables(width_x)
    all_tables = (cos_y, sin_y, cos_x, sin_x)
    slow_planes = jnp.concatenate([slowness, slowness], axis=0)
    slow_refs = jnp.concatenate([ref_slow, ref_slow], axis=0)
    mult_real, mult_imag, corr_real, corr_imag = media_factors(
        slow_planes, slow_refs, lat_count, lat_index
    )
    for _ in range(TICKS):
        joined_real = jnp.concatenate([down_real, up_real], axis=0)
        joined_imag = jnp.concatenate([down_imaginary, up_imaginary], axis=0)
        prop_real, prop_imag = spectral(
            joined_real,
            joined_imag,
            mult_real,
            mult_imag,
            corr_real,
            corr_imag,
            all_tables,
            lat_count,
        )
        above_real, above_imag = passed_along(
            (prop_real[levels - 1], prop_imag[levels - 1]), "depth", 1
        )
        below_real, below_imag = passed_along((prop_real[levels], prop_imag[levels]), "depth", -1)
        head_real = above_real + top_mask * source_real
        head_imag = above_imag + top_mask * source_imaginary
        in_down_real = jnp.concatenate([head_real[None], prop_real[: levels - 1]], axis=0)
        in_down_imag = jnp.concatenate([head_imag[None], prop_imag[: levels - 1]], axis=0)
        in_up_real = jnp.concatenate([prop_real[levels + 1 :], below_real[None]], axis=0)
        in_up_imag = jnp.concatenate([prop_imag[levels + 1 :], below_imag[None]], axis=0)
        down_real = in_down_real - reflectivity * in_up_real
        down_imaginary = in_down_imag - reflectivity * in_up_imag
        up_real = in_up_real + reflectivity * in_down_real
        up_imaginary = in_up_imag + reflectivity * in_down_imag
    return (down_real, down_imaginary, up_real, up_imaginary)


def path_at(section, place, pairs):
    place = place if section % 2 == 0 else pairs - 1 - place
    return place ^ (place >> 1)


def place_on(section, pair, pairs):
    shift, place = 1, pair
    while (1 << shift) <= pairs:
        place = place ^ (pair >> shift)
        shift += 1
    return jnp.where(section % 2 == 0, place, pairs - 1 - place)


def level_pairs(sections, pairs, parity):
    where = [
        g * pairs * 2 + path_at(g, l, pairs) * 2 for g in range(sections) for l in range(pairs)
    ]
    edges = []
    for z in range(parity, len(where) - 1, 2):
        for core in range(2):
            here, below = where[z] + core, where[z + 1] + core
            edges += [(here, below), (below, here)]
    return edges


def section_pairs(sections, pairs, parity):
    width = 2 * pairs
    edges = []
    for g in range(parity, sections - 1, 2):
        for n in range(width):
            edges += [(g * width + n, (g + 1) * width + n), ((g + 1) * width + n, g * width + n)]
    return edges


def split_table(table):
    high = table.astype(np.float32).astype(jnp.bfloat16)
    return high, (table - high.astype(np.float64)).astype(np.float32).astype(jnp.bfloat16)


def half_tables(order, inverse):
    count = len(order)
    angle = (np.arange(count)[None, :] * np.asarray(order)[:, None] % count) * (
        2.0 * math.pi / count
    )
    if inverse:
        angle = angle.T
    (cos_high, cos_low), (sin_high, sin_low) = split_table(np.cos(angle)), split_table(
        np.sin(angle) * (-1.0 if inverse else 1.0)
    )
    real = [np.concatenate([c, -s], axis=1) for c, s in ((cos_high, sin_high), (cos_low, sin_low))]
    imag = [np.concatenate([s, c], axis=1) for c, s in ((cos_high, sin_high), (cos_low, sin_low))]
    return np.concatenate([real[0], real[0], real[1], imag[0], imag[0], imag[1]], axis=0)


def turn_tables(order):
    angle = np.asarray(order) * (math.pi / len(order))
    return np.stack([np.cos(angle), np.sin(angle)]).astype(np.float32)


def halves(value):
    high = value.astype(jnp.bfloat16)
    low = (value - high.astype(jnp.float32)).astype(jnp.bfloat16)
    return high, low


def cos_sin(angle):
    square = angle * angle
    sine = 1.0
    for n in (13, 11, 9, 7, 5, 3):
        scale = -1.0 / (n * (n - 1))
        sine = 1.0 + square * (scale * sine)
    cosine = 1.0
    for n in (14, 12, 10, 8, 6, 4, 2):
        scale = -1.0 / (n * (n - 1))
        cosine = 1.0 + square * (scale * cosine)
    return cosine, angle * sine


def multiplier(ref, rows, columns, core):
    shape = (rows // 2, columns)
    along = lax.broadcasted_iota(jnp.int32, shape, 1)
    odd = (along >= columns // 2).astype(jnp.int32)

    def wave(count, index):
        folded = jnp.where(index < count // 2, index, index - count)
        return folded.astype(jnp.float32) * (2.0 * math.pi / count)

    wave_x = wave(rows, 2 * lax.broadcasted_iota(jnp.int32, shape, 0) + odd)
    wave_y = wave(columns, 2 * (along - odd * (columns // 2)) + core)
    argument = (OMEGA * ref) ** 2 - (wave_x * wave_x + wave_y * wave_y)
    vertical = jnp.sqrt(jnp.maximum(argument, 0.0)) * DEPTH_STEP
    evanescent = jnp.sqrt(jnp.maximum(-argument, 0.0)) * DEPTH_STEP
    factor = jnp.exp(-evanescent) * (1.0 / (rows * columns))
    cosine, sine = cos_sin(0.5 * vertical)
    return factor * (1.0 - 2.0 * sine * sine), factor * (-2.0 * sine * cosine)


def parts_of(a, b, axis):
    a_high, a_low = halves(a)
    b_high, b_low = halves(b)
    return jnp.concatenate([a_high, a_low, a_high, b_high, b_low, b_high], axis=axis)


def forward_y(real, imag, table, turn):
    count, wide = real.shape[0], real.shape[1] // 2
    cosine, sine = turn[0:1, :], turn[1:2, :]
    d_real, d_imag = real[:, :wide] - real[:, wide:], imag[:, :wide] - imag[:, wide:]
    a = jnp.concatenate(
        [real[:, :wide] + real[:, wide:], d_real * cosine + d_imag * sine], axis=0
    )
    b = jnp.concatenate(
        [imag[:, :wide] + imag[:, wide:], d_imag * cosine - d_real * sine], axis=0
    )
    out = jnp.dot(parts_of(a, b, 1), table[...], preferred_element_type=jnp.float32)
    return (out[:count, :wide], out[:count, wide:]), (out[count:, :wide], out[count:, wide:])


def inverse_y(a, b, table, turn):
    count, wide = a.shape[0] // 2, a.shape[1]
    cosine, sine = turn[0:1, :], turn[1:2, :]
    out = jnp.dot(parts_of(a, b, 1), table[...], preferred_element_type=jnp.float32)
    e_real, e_imag = out[:count, :wide], out[:count, wide:]
    o_real, o_imag = out[count:, :wide], out[count:, wide:]
    o_real, o_imag = o_real * cosine - o_imag * sine, o_imag * cosine + o_real * sine
    return (
        jnp.concatenate([e_real + o_real, e_real - o_real], axis=1),
        jnp.concatenate([e_imag + o_imag, e_imag - o_imag], axis=1),
    )


class Place:
    def __init__(self, pairs):
        index = lax.axis_index("lat")
        self.section = lax.axis_index("depth")
        self.pair = index // 2
        self.core = index % 2
        self.level = place_on(self.section, self.pair, pairs)
        self.first = self.level == 0
        self.last = self.level == pairs - 1


def local_call(body, out_shapes, spaces, scratch=(), limit=24 << 20):
    memory = {"v": pltpu.VMEM, "s": pltpu.SMEM, "h": pltpu.HBM}
    return pl.pallas_call(
        body,
        out_shape=[jax.ShapeDtypeStruct(shape, jnp.float32) for shape in out_shapes],
        in_specs=[pl.BlockSpec(memory_space=memory[space]) for space in spaces],
        out_specs=[pl.BlockSpec(memory_space=pltpu.VMEM) for _ in out_shapes],
        scratch_shapes=list(scratch),
        compiler_params=pltpu.CompilerParams(vmem_limit_bytes=limit),
    )


def plane_shards(
    down_real,
    down_imaginary,
    up_real,
    up_imaginary,
    slowness,
    ref_slow,
    reflectivity,
    source_real,
    source_imaginary,
):
    levels, block, columns = down_real.shape
    sections = lax.axis_size("depth")
    lat_count = lax.axis_size("lat")
    pairs = lat_count // 2
    rows = block * lat_count
    tall = rows // 2
    wide = columns // 2
    two, four = 2 * block, 4 * block
    swap = [(index, index ^ 1) for index in range(lat_count)]
    quarter = tall // 2
    place = np.arange(tall)
    order = place % quarter // block * two + place // quarter * block + place % block
    straight = np.arange(wide)
    y_table, y_back = (jnp.asarray(half_tables(straight, inverse)) for inverse in (False, True))
    x_table, x_back = (jnp.asarray(half_tables(order, inverse).T) for inverse in (False, True))
    y_turn = jnp.asarray(turn_tables(straight))
    x_turn = jnp.asarray(
        np.broadcast_to(turn_tables(order)[:, :, None], (2, tall, wide)).copy()
    )
    f32 = jnp.float32
    local = (2 * tall, columns)
    part = (2 * tall, wide)

    def across(step):
        return [(index, index ^ (2 * step)) for index in range(lat_count)]

    def top(here):
        return here.first & (here.section == 0)

    def split_body(dr, di, ur, ui, slow, refl, sr, si, *rest):
        planes, media, sems = rest[:pairs], rest[pairs : 2 * pairs], rest[2 * pairs]
        here = Place(pairs)

        def pieces(step, first, second):
            level = place_on(here.section, here.pair ^ step, pairs)
            out = []
            for n, array in enumerate(first + second):
                source = array if len(array.shape) == 2 else array.at[level]
                out.append((source, planes[step].at[pl.ds(n * block, block), :]))
            out.append((slow.at[level], media[step].at[pl.ds(0, block), :]))
            out.append((refl.at[level], media[step].at[pl.ds(block, block), :]))
            return [
                pltpu.make_async_copy(source, target, sems.at[step * 6 + n])
                for n, (source, target) in enumerate(out)
            ]

        def each(act):
            for step in range(pairs):
                level = place_on(here.section, here.pair ^ step, pairs)
                sourced = (level == 0) & (here.section == 0)

                @pl.when(sourced)
                def _():
                    for move in pieces(step, (dr, di), (sr, si)):
                        act(move)

                @pl.when((level % 2 == 0) & jnp.logical_not(sourced))
                def _():
                    for move in pieces(step, (dr, di), (ur, ui)):
                        act(move)

                @pl.when(level % 2 == 1)
                def _():
                    for move in pieces(step, (ur, ui), (dr, di)):
                        act(move)

        each(lambda move: move.start())
        each(lambda move: move.wait())

    outs = local_call(
        split_body,
        [(four, columns)] * pairs + [(two, columns)] * pairs,
        "h" * 8,
        [pltpu.SemaphoreType.DMA((6 * pairs,))],
    )(
        *(
            pltpu.with_memory_space_constraint(array, pltpu.HBM)
            for array in (
                down_real,
                down_imaginary,
                up_real,
                up_imaginary,
                slowness,
                reflectivity,
                source_real,
                source_imaginary,
            )
        )
    )

    def exchanged(pieces):
        moved = [pieces[0]]
        for step in range(1, pairs):
            moved.append(lax.ppermute(pieces[step], "lat", across(step)))
        return moved

    planes = exchanged(outs[:pairs])
    media = exchanged(outs[pairs:])

    def multiplier_body(ref_slow, out):
        here = Place(pairs)
        out[:tall], out[tall:] = multiplier(ref_slow[here.level], rows, columns, here.core)

    mult = local_call(multiplier_body, [local], "s")(ref_slow)[0]

    def media_body(*refs):
        pieces, ref_slow, corr, refl = refs[:pairs], refs[pairs], refs[pairs + 1], refs[pairs + 2]
        here = Place(pairs)
        ref = ref_slow[here.level]
        for step in range(pairs):
            start = (here.pair ^ step) * block
            theta = (pieces[step][pl.ds(0, block), :] - ref) * (OMEGA * DEPTH_STEP)
            cosine, sine = cos_sin(theta)
            corr[pl.ds(pl.multiple_of(start, block), block), :] = cosine
            corr[pl.ds(pl.multiple_of(tall + start, block), block), :] = sine
            refl[pl.ds(pl.multiple_of(start, block), block), :] = pieces[step][
                pl.ds(block, block), :
            ]

    corr, refl = local_call(media_body, [local, (tall, columns)], "v" * pairs + "s")(
        *media, ref_slow
    )

    def shared(first, second, here, keep, send):
        def put(mine, theirs):
            keep[:tall], keep[tall:] = mine
            send[:tall], send[tall:] = theirs

        @pl.when(here.core == 0)
        def _():
            put(first, second)

        @pl.when(here.core == 1)
        def _():
            put(second, first)

    def enter(which):
        def body(*refs):
            pieces, (table, turn, keep, send, whole) = refs[:pairs], refs[pairs:]
            here = Place(pairs)
            for step in range(pairs):
                start = (here.pair ^ step) * block
                for n in range(2):
                    whole[pl.ds(pl.multiple_of(n * tall + start, block), block), :] = pieces[step][
                        pl.ds((2 * which + n) * block, block), :
                    ]
            shared(*forward_y(whole[:tall], whole[tall:], table, turn), here, keep, send)

        return local_call(body, [part, part, local], "v" * (pairs + 2))(*planes, y_table, y_turn)

    def mixed(which, ahead, behind, source):
        def body(ahead, behind, source, refl, table, turn, keep, send):
            here = Place(pairs)
            sign = jnp.where((here.level % 2 == 0) == (which == 0), -1.0, 1.0)
            behind = jnp.where(top(here), source[...], behind[...])
            base, side = (behind, ahead[...]) if which == 0 else (ahead[...], behind)
            weight = refl[...] * sign
            real = base[:tall] + weight * side[:tall]
            imag = base[tall:] + weight * side[tall:]
            shared(*forward_y(real, imag, table, turn), here, keep, send)

        return local_call(body, [part, part], "v" * 6)(ahead, behind, source, refl, y_table, y_turn)

    def column(keep, got):
        def body(keep, got, mult, table, back, turn, out, send, near, far):
            here = Place(pairs)
            for piece, core in ((keep, here.core), (got, 1 - here.core)):
                for n in range(2):
                    take = pl.ds(pl.multiple_of(n * tall + core * quarter, quarter), quarter)
                    near[take, :] = piece[pl.ds(n * tall, quarter), :]
                    far[take, :] = piece[pl.ds(n * tall + quarter, quarter), :]
            cosine, sine = turn[0], turn[1]
            d_real, d_imag = near[:tall] - far[:tall], near[tall:] - far[tall:]
            a = jnp.concatenate(
                [near[:tall] + far[:tall], d_real * cosine + d_imag * sine], axis=1
            )
            b = jnp.concatenate(
                [near[tall:] + far[tall:], d_imag * cosine - d_real * sine], axis=1
            )
            spec = jnp.dot(table[...], parts_of(a, b, 0), preferred_element_type=f32)
            a = spec[:tall] * mult[:tall] - spec[tall:] * mult[tall:]
            b = spec[:tall] * mult[tall:] + spec[tall:] * mult[:tall]
            moved = jnp.dot(back[...], parts_of(a, b, 0), preferred_element_type=f32)
            o_real, o_imag = moved[:tall, wide:], moved[tall:, wide:]
            o_real, o_imag = o_real * cosine - o_imag * sine, o_imag * cosine + o_real * sine
            e_real, e_imag = moved[:tall, :wide], moved[tall:, :wide]
            joined = []
            for even, odd in ((e_real, o_real), (e_imag, o_imag)):
                low, high = even + odd, even - odd
                joined.append(
                    [
                        jnp.concatenate([low[take], high[take]], axis=0)
                        for take in (slice(0, quarter), slice(quarter, tall))
                    ]
                )
            shared(*zip(*joined), here, out, send)

        return local_call(
            body, [part, part], "v" * 6, [pltpu.VMEM(part, f32) for _ in range(2)]
        )(keep, got, mult, x_table, x_back, x_turn)

    def corrected(keep, got, corr, table, turn, here, whole):
        for piece, core in ((keep, here.core), (got, 1 - here.core)):
            take = pl.ds(pl.multiple_of(core * tall, tall), tall)
            whole[take, pl.ds(0, wide)] = piece[:tall]
            whole[take, pl.ds(wide, wide)] = piece[tall:]
        real, imag = inverse_y(whole[:, :wide], whole[:, wide:], table, turn)
        cosine, sine = corr[:tall], corr[tall:]
        return real * cosine + imag * sine, imag * cosine - real * sine

    def leave(keep, got, *held):
        def body(keep, got, corr, *refs):
            kept, (table, turn), outs = refs[: len(held)], refs[len(held) :][:2], refs[2 + len(held) :]
            whole = outs[-1]
            for source, target in zip(kept, outs[1:]):
                target[...] = source[...]
            real, imag = corrected(keep, got, corr, table, turn, Place(pairs), whole)
            outs[0][:tall], outs[0][tall:] = real, imag

        return local_call(
            body, [local] * (1 + len(held)), "v" * (5 + len(held)), [pltpu.VMEM(local, f32)]
        )(keep, got, corr, *held, y_back, y_turn)

    def leave_last(keep, got):
        def body(keep, got, corr, table, turn, *refs):
            outs, whole = refs[:pairs], refs[pairs]
            here = Place(pairs)
            real, imag = corrected(keep, got, corr, table, turn, here, whole)
            whole[:tall], whole[tall:] = real, imag
            for step in range(pairs):
                start = (here.pair ^ step) * block
                for m in range(2):
                    outs[step][pl.ds(m * block, block), :] = whole[
                        pl.ds(pl.multiple_of(m * tall + start, block), block), :
                    ]

        return local_call(
            body, [(two, columns)] * pairs, "v" * 5, [pltpu.VMEM(local, f32)]
        )(keep, got, corr, y_back, y_turn)

    def crossed(value):
        return lax.ppermute(value, "lat", swap)

    keep0, send0, _ = enter(0)
    got0 = crossed(send0)
    keep1, send1, source = enter(1)
    got1 = crossed(send1)
    for _ in range(TICKS - 1):
        keep0, send0 = column(keep0, got0)
        got0 = crossed(send0)
        keep1, send1 = column(keep1, got1)
        got1 = crossed(send1)
        first = leave(keep0, got0)[0]
        second, first = leave(keep1, got1, first)
        ahead = lax.ppermute(first, ("depth", "lat"), level_pairs(sections, pairs, 0))
        behind = lax.ppermute(second, ("depth", "lat"), level_pairs(sections, pairs, 1))
        keep1, send1 = mixed(1, ahead, behind, source)
        got1 = crossed(send1)
        keep0, send0 = mixed(0, ahead, behind, source)
        got0 = crossed(send0)
    keep1, send1 = column(keep1, got1)
    got1 = crossed(send1)
    keep0, send0 = column(keep0, got0)
    got0 = crossed(send0)
    back1 = exchanged(leave_last(keep1, got1))
    leaving = leave_last(keep0, got0)
    back0 = exchanged(leaving)

    def pick_body(*refs):
        pieces, even, odd = refs[:pairs], refs[pairs], refs[pairs + 1]
        here = Place(pairs)
        for step in range(pairs):
            level = place_on(here.section, here.pair ^ step, pairs)
            for edge, mine in ((pairs - 1, 0), (0, 1)):
                for target, parity in ((even, mine), (odd, 1 - mine)):

                    @pl.when((level == edge) & (here.section % 2 == parity))
                    def _():
                        target[...] = pieces[step][...]

    even, odd = local_call(pick_body, [(two, columns)] * 2, "v" * pairs)(*back1)
    even = lax.ppermute(even, ("depth", "lat"), section_pairs(sections, pairs, 0))
    odd = lax.ppermute(odd, ("depth", "lat"), section_pairs(sections, pairs, 1))

    def mix_body(*refs):
        first, second = refs[:pairs], refs[pairs : 2 * pairs]
        even, odd, refl, sr, si = refs[2 * pairs : 2 * pairs + 5]
        dr, di, ur, ui, down, up = refs[2 * pairs + 5 :]
        here = Place(pairs)
        for step in range(pairs):
            level = place_on(here.section, here.pair ^ step, pairs)
            below, above = (level + 1) % levels, (level + levels - 1) % levels

            @pl.when(level % 2 == 0)
            def _():
                down[below] = first[step][...]
                up[above] = second[step][...]

            @pl.when(level % 2 == 1)
            def _():
                down[below] = second[step][...]
                up[above] = first[step][...]

        @pl.when(here.section % 2 == 0)
        def _():
            down[0] = odd[...]
            up[levels - 1] = even[...]

        @pl.when(here.section % 2 == 1)
        def _():
            down[0] = even[...]
            up[levels - 1] = odd[...]

        @pl.when(here.section == 0)
        def _():
            down[0, pl.ds(0, block), :] = sr[...]
            down[0, pl.ds(block, block), :] = si[...]

        for n in range(levels):
            r = refl[n]
            d_real, d_imag = down[n, pl.ds(0, block), :], down[n, pl.ds(block, block), :]
            u_real, u_imag = up[n, pl.ds(0, block), :], up[n, pl.ds(block, block), :]
            dr[n] = d_real - r * u_real
            di[n] = d_imag - r * u_imag
            ur[n] = u_real + r * d_real
            ui[n] = u_imag + r * d_imag

    return tuple(
        local_call(
            mix_body,
            [(levels, block, columns)] * 4,
            "v" * (2 * pairs + 5),
            [pltpu.VMEM((levels, two, columns), f32) for _ in range(2)],
        )(*back0, *back1, even, odd, reflectivity, source_real, source_imaginary)
    )


def fits(shape, mesh):
    levels, rows, columns = shape
    levels = levels // mesh.shape["depth"]
    return (
        mesh.shape["lat"] == 2 * levels
        and levels >= 2
        and levels & (levels - 1) == 0
        and rows // mesh.shape["lat"] % 16 == 0
        and columns % 256 == 0
    )


def solution(mesh):
    rows = P("depth", "lat", None)
    placed = (rows,) * 5 + (P("depth"), rows, P("lat", None), P("lat", None))

    def mapped(body):
        return jax.shard_map(
            body, mesh=mesh, in_specs=placed, out_specs=(rows,) * 4, check_vma=False
        )

    by_planes = mapped(plane_shards)
    by_rows = mapped(row_shards)

    def run(*arrays):
        return (by_planes if fits(arrays[0].shape, mesh) else by_rows)(*arrays)

    return run
```

```python
import math

import jax
import jax.numpy as jnp
import numpy as np
from jax import lax
from jax.experimental import pallas as pl
from jax.experimental.pallas import tpu as pltpu
from jax.sharding import PartitionSpec as P


TICKS = 3

OMEGA = 2.5
DEPTH_STEP = 1.0


def passed_along(value, axis, steps):
    count = lax.axis_size(axis)
    initial, last = (max(0, -steps), min(count, count - steps))
    return lax.ppermute(value, axis, [(source, source + steps) for source in range(initial, last)])


def tables(count):
    index = jnp.arange(count, dtype=jnp.int32)
    phase = index[:, None] * index[None, :] % count
    angle = phase.astype(jnp.float32) * (2.0 * math.pi / count)
    return (jnp.cos(angle), jnp.sin(angle))


def wrapped_numbers(index, count):
    folded = jnp.where(index < count // 2, index, index - count)
    return folded.astype(jnp.float32) * (2.0 * math.pi / count)


def complex_product(form, real, imag, cosine, sine, inverse):
    real_cos = jnp.einsum(form, real, cosine, precision=lax.Precision.HIGHEST)
    real_sin = jnp.einsum(form, real, sine, precision=lax.Precision.HIGHEST)
    imag_cos = jnp.einsum(form, imag, cosine, precision=lax.Precision.HIGHEST)
    imag_sin = jnp.einsum(form, imag, sine, precision=lax.Precision.HIGHEST)
    if inverse:
        return (real_cos - imag_sin, imag_cos + real_sin)
    return (real_cos + imag_sin, imag_cos - real_sin)


def spectral(real, imag, mult_real, mult_imag, corr_real, corr_imag, all_tables, lat_count):
    cos_y, sin_y, cos_x, sin_x = all_tables
    planes = real.shape[0]
    rows_here = real.shape[1]
    width_y = real.shape[2]
    width_x = rows_here * lat_count
    cols_here = width_y // lat_count
    first_real, first_imag = complex_product("nxy,yk->xkn", real, imag, cos_y, sin_y, False)
    send_real = jnp.swapaxes(
        first_real.reshape(rows_here, lat_count, cols_here, planes), 0, 1
    ).reshape(lat_count, rows_here * cols_here * planes)
    send_imag = jnp.swapaxes(
        first_imag.reshape(rows_here, lat_count, cols_here, planes), 0, 1
    ).reshape(lat_count, rows_here * cols_here * planes)
    got_real, got_imag = (
        lax.all_to_all(send_real, "lat", split_axis=0, concat_axis=0, tiled=True),
        lax.all_to_all(send_imag, "lat", split_axis=0, concat_axis=0, tiled=True),
    )
    got_real = got_real.reshape(width_x, cols_here, planes)
    got_imag = got_imag.reshape(width_x, cols_here, planes)
    spec_real, spec_imag = complex_product("xqn,xp->nqp", got_real, got_imag, cos_x, sin_x, False)
    moved_real = spec_real * mult_real - spec_imag * mult_imag
    moved_imag = spec_real * mult_imag + spec_imag * mult_real
    back_real, back_imag = complex_product(
        "nqp,px->qxn", moved_real, moved_imag, cos_x, sin_x, True
    )
    back_real = jnp.swapaxes(
        (back_real / width_x).reshape(cols_here, lat_count, rows_here, planes), 0, 1
    ).reshape(lat_count, cols_here * rows_here * planes)
    back_imag = jnp.swapaxes(
        (back_imag / width_x).reshape(cols_here, lat_count, rows_here, planes), 0, 1
    ).reshape(lat_count, cols_here * rows_here * planes)
    ret_real, ret_imag = (
        lax.all_to_all(back_real, "lat", split_axis=0, concat_axis=0, tiled=True),
        lax.all_to_all(back_imag, "lat", split_axis=0, concat_axis=0, tiled=True),
    )
    ret_real = ret_real.reshape(width_y, rows_here, planes)
    ret_imag = ret_imag.reshape(width_y, rows_here, planes)
    plane_real, plane_imag = complex_product("kxn,ky->nxy", ret_real, ret_imag, cos_y, sin_y, True)
    plane_real = plane_real / width_y
    plane_imag = plane_imag / width_y
    final_real = plane_real * corr_real - plane_imag * corr_imag
    final_imag = plane_real * corr_imag + plane_imag * corr_real
    return (final_real, final_imag)


def media_factors(slow_planes, slow_refs, lat_count, lat_index):
    rows_here = slow_planes.shape[1]
    width_y = slow_planes.shape[2]
    width_x = rows_here * lat_count
    cols_here = width_y // lat_count
    wave_x = wrapped_numbers(jnp.arange(width_x, dtype=jnp.int32), width_x)
    wave_y = wrapped_numbers(
        lat_index * cols_here + jnp.arange(cols_here, dtype=jnp.int32), width_y
    )
    squared = wave_y[:, None] ** 2 + wave_x[None, :] ** 2
    argument = (OMEGA * slow_refs[:, None, None]) ** 2 - squared[None]
    vertical = jnp.sqrt(jnp.maximum(argument, 0.0)) * DEPTH_STEP
    evanescent = jnp.sqrt(jnp.maximum(-argument, 0.0)) * DEPTH_STEP
    factor = jnp.exp(-evanescent)
    theta = OMEGA * (slow_planes - slow_refs[:, None, None]) * DEPTH_STEP
    return (
        factor * jnp.cos(vertical),
        -factor * jnp.sin(vertical),
        jnp.cos(theta),
        -jnp.sin(theta),
    )


def row_shards(
    down_real,
    down_imaginary,
    up_real,
    up_imaginary,
    slowness,
    ref_slow,
    reflectivity,
    source_real,
    source_imaginary,
):
    levels = down_real.shape[0]
    lat_count = lax.axis_size("lat")
    lat_index = lax.axis_index("lat")
    top_mask = (lax.axis_index("depth") == 0).astype(jnp.float32)
    width_x = down_real.shape[1] * lat_count
    cos_y, sin_y = tables(down_real.shape[2])
    cos_x, sin_x = tables(width_x)
    all_tables = (cos_y, sin_y, cos_x, sin_x)
    slow_planes = jnp.concatenate([slowness, slowness], axis=0)
    slow_refs = jnp.concatenate([ref_slow, ref_slow], axis=0)
    mult_real, mult_imag, corr_real, corr_imag = media_factors(
        slow_planes, slow_refs, lat_count, lat_index
    )
    for _ in range(TICKS):
        joined_real = jnp.concatenate([down_real, up_real], axis=0)
        joined_imag = jnp.concatenate([down_imaginary, up_imaginary], axis=0)
        prop_real, prop_imag = spectral(
            joined_real,
            joined_imag,
            mult_real,
            mult_imag,
            corr_real,
            corr_imag,
            all_tables,
            lat_count,
        )
        above_real, above_imag = passed_along(
            (prop_real[levels - 1], prop_imag[levels - 1]), "depth", 1
        )
        below_real, below_imag = passed_along((prop_real[levels], prop_imag[levels]), "depth", -1)
        head_real = above_real + top_mask * source_real
        head_imag = above_imag + top_mask * source_imaginary
        in_down_real = jnp.concatenate([head_real[None], prop_real[: levels - 1]], axis=0)
        in_down_imag = jnp.concatenate([head_imag[None], prop_imag[: levels - 1]], axis=0)
        in_up_real = jnp.concatenate([prop_real[levels + 1 :], below_real[None]], axis=0)
        in_up_imag = jnp.concatenate([prop_imag[levels + 1 :], below_imag[None]], axis=0)
        down_real = in_down_real - reflectivity * in_up_real
        down_imaginary = in_down_imag - reflectivity * in_up_imag
        up_real = in_up_real + reflectivity * in_down_real
        up_imaginary = in_up_imag + reflectivity * in_down_imag
    return (down_real, down_imaginary, up_real, up_imaginary)


def path_at(section, place, pairs):
    place = place if section % 2 == 0 else pairs - 1 - place
    return place ^ (place >> 1)


def place_on(section, pair, pairs):
    shift, place = 1, pair
    while (1 << shift) <= pairs:
        place = place ^ (pair >> shift)
        shift += 1
    return jnp.where(section % 2 == 0, place, pairs - 1 - place)


def level_pairs(sections, pairs, parity):
    where = [
        g * pairs * 2 + path_at(g, l, pairs) * 2 for g in range(sections) for l in range(pairs)
    ]
    edges = []
    for z in range(parity, len(where) - 1, 2):
        for core in range(2):
            here, below = where[z] + core, where[z + 1] + core
            edges += [(here, below), (below, here)]
    return edges


def section_pairs(sections, pairs, parity):
    width = 2 * pairs
    edges = []
    for g in range(parity, sections - 1, 2):
        for n in range(width):
            edges += [(g * width + n, (g + 1) * width + n), ((g + 1) * width + n, g * width + n)]
    return edges


def split_table(table):
    high = table.astype(np.float32).astype(jnp.bfloat16)
    return high, (table - high.astype(np.float64)).astype(np.float32).astype(jnp.bfloat16)


def half_tables(order, inverse):
    count = len(order)
    angle = (np.arange(count)[None, :] * np.asarray(order)[:, None] % count) * (
        2.0 * math.pi / count
    )
    if inverse:
        angle = angle.T
    (cos_high, cos_low), (sin_high, sin_low) = split_table(np.cos(angle)), split_table(
        np.sin(angle) * (-1.0 if inverse else 1.0)
    )
    real = [np.concatenate([c, -s], axis=1) for c, s in ((cos_high, sin_high), (cos_low, sin_low))]
    imag = [np.concatenate([s, c], axis=1) for c, s in ((cos_high, sin_high), (cos_low, sin_low))]
    return np.concatenate([real[0], real[0], real[1], imag[0], imag[0], imag[1]], axis=0)


def turn_tables(order):
    angle = np.asarray(order) * (math.pi / len(order))
    return np.stack([np.cos(angle), np.sin(angle)]).astype(np.float32)


def halves(value):
    high = value.astype(jnp.bfloat16)
    low = (value - high.astype(jnp.float32)).astype(jnp.bfloat16)
    return high, low


def cos_sin(angle):
    square = angle * angle
    sine = 1.0
    for n in (13, 11, 9, 7, 5, 3):
        scale = -1.0 / (n * (n - 1))
        sine = 1.0 + square * (scale * sine)
    cosine = 1.0
    for n in (14, 12, 10, 8, 6, 4, 2):
        scale = -1.0 / (n * (n - 1))
        cosine = 1.0 + square * (scale * cosine)
    return cosine, angle * sine


def multiplier(ref, rows, columns, core):
    shape = (rows // 2, columns)
    along = lax.broadcasted_iota(jnp.int32, shape, 1)
    odd = (along >= columns // 2).astype(jnp.int32)

    def wave(count, index):
        folded = jnp.where(index < count // 2, index, index - count)
        return folded.astype(jnp.float32) * (2.0 * math.pi / count)

    wave_x = wave(rows, 2 * lax.broadcasted_iota(jnp.int32, shape, 0) + odd)
    wave_y = wave(columns, 2 * (along - odd * (columns // 2)) + core)
    argument = (OMEGA * ref) ** 2 - (wave_x * wave_x + wave_y * wave_y)
    vertical = jnp.sqrt(jnp.maximum(argument, 0.0)) * DEPTH_STEP
    evanescent = jnp.sqrt(jnp.maximum(-argument, 0.0)) * DEPTH_STEP
    factor = jnp.exp(-evanescent) * (1.0 / (rows * columns))
    cosine, sine = cos_sin(0.5 * vertical)
    return factor * (1.0 - 2.0 * sine * sine), factor * (-2.0 * sine * cosine)


def parts_of(a, b, axis):
    a_high, a_low = halves(a)
    b_high, b_low = halves(b)
    return jnp.concatenate([a_high, a_low, a_high, b_high, b_low, b_high], axis=axis)


def forward_y(real, imag, table, turn):
    count, wide = real.shape[0], real.shape[1] // 2
    cosine, sine = turn[0:1, :], turn[1:2, :]
    d_real, d_imag = real[:, :wide] - real[:, wide:], imag[:, :wide] - imag[:, wide:]
    a = jnp.concatenate(
        [real[:, :wide] + real[:, wide:], d_real * cosine + d_imag * sine], axis=0
    )
    b = jnp.concatenate(
        [imag[:, :wide] + imag[:, wide:], d_imag * cosine - d_real * sine], axis=0
    )
    out = jnp.dot(parts_of(a, b, 1), table[...], preferred_element_type=jnp.float32)
    return (out[:count, :wide], out[:count, wide:]), (out[count:, :wide], out[count:, wide:])


def inverse_y(a, b, table, turn):
    count, wide = a.shape[0] // 2, a.shape[1]
    cosine, sine = turn[0:1, :], turn[1:2, :]
    out = jnp.dot(parts_of(a, b, 1), table[...], preferred_element_type=jnp.float32)
    e_real, e_imag = out[:count, :wide], out[:count, wide:]
    o_real, o_imag = out[count:, :wide], out[count:, wide:]
    o_real, o_imag = o_real * cosine - o_imag * sine, o_imag * cosine + o_real * sine
    return (
        jnp.concatenate([e_real + o_real, e_real - o_real], axis=1),
        jnp.concatenate([e_imag + o_imag, e_imag - o_imag], axis=1),
    )


class Place:
    def __init__(self, pairs):
        index = lax.axis_index("lat")
        self.section = lax.axis_index("depth")
        self.pair = index // 2
        self.core = index % 2
        self.level = place_on(self.section, self.pair, pairs)
        self.first = self.level == 0
        self.last = self.level == pairs - 1


def local_call(body, out_shapes, spaces, scratch=(), limit=24 << 20):
    memory = {"v": pltpu.VMEM, "s": pltpu.SMEM, "h": pltpu.HBM}
    return pl.pallas_call(
        body,
        out_shape=[
            jax.ShapeDtypeStruct(shape, jnp.float32) if isinstance(shape, tuple) else shape
            for shape in out_shapes
        ],
        in_specs=[pl.BlockSpec(memory_space=memory[space]) for space in spaces],
        out_specs=[pl.BlockSpec(memory_space=pltpu.VMEM) for _ in out_shapes],
        scratch_shapes=list(scratch),
        compiler_params=pltpu.CompilerParams(vmem_limit_bytes=limit),
    )


def plane_shards(
    down_real,
    down_imaginary,
    up_real,
    up_imaginary,
    slowness,
    ref_slow,
    reflectivity,
    source_real,
    source_imaginary,
):
    levels, block, columns = down_real.shape
    sections = lax.axis_size("depth")
    lat_count = lax.axis_size("lat")
    pairs = lat_count // 2
    rows = block * lat_count
    tall = rows // 2
    wide = columns // 2
    two, four = 2 * block, 4 * block
    swap = [(index, index ^ 1) for index in range(lat_count)]
    quarter = tall // 2
    place = np.arange(tall)
    order = place % quarter // block * two + place // quarter * block + place % block
    straight = np.arange(wide)
    y_table, y_back = (jnp.asarray(half_tables(straight, inverse)) for inverse in (False, True))
    x_table, x_back = (jnp.asarray(half_tables(order, inverse).T) for inverse in (False, True))
    y_turn = jnp.asarray(turn_tables(straight))
    x_turn = jnp.asarray(
        np.broadcast_to(turn_tables(order)[:, :, None], (2, tall, wide)).copy()
    )
    f32 = jnp.float32
    local = (2 * tall, columns)
    part = (2 * tall, wide)

    def across(step):
        return [(index, index ^ (2 * step)) for index in range(lat_count)]

    def top(here):
        return here.first & (here.section == 0)

    def split_body(dr, di, ur, ui, slow, refl, sr, si, *rest):
        planes, media, sems = rest[:pairs], rest[pairs : 2 * pairs], rest[2 * pairs]
        here = Place(pairs)

        def pieces(step, first, second):
            level = place_on(here.section, here.pair ^ step, pairs)
            out = []
            for n, array in enumerate(first + second):
                source = array if len(array.shape) == 2 else array.at[level]
                out.append((source, planes[step].at[pl.ds(n * block, block), :]))
            out.append((slow.at[level], media[step].at[pl.ds(0, block), :]))
            out.append((refl.at[level], media[step].at[pl.ds(block, block), :]))
            return [
                pltpu.make_async_copy(source, target, sems.at[step * 6 + n])
                for n, (source, target) in enumerate(out)
            ]

        def each(act):
            for step in range(pairs):
                level = place_on(here.section, here.pair ^ step, pairs)
                sourced = (level == 0) & (here.section == 0)

                @pl.when(sourced)
                def _():
                    for move in pieces(step, (dr, di), (sr, si)):
                        act(move)

                @pl.when((level % 2 == 0) & jnp.logical_not(sourced))
                def _():
                    for move in pieces(step, (dr, di), (ur, ui)):
                        act(move)

                @pl.when(level % 2 == 1)
                def _():
                    for move in pieces(step, (ur, ui), (dr, di)):
                        act(move)

        each(lambda move: move.start())
        each(lambda move: move.wait())

    outs = local_call(
        split_body,
        [(four, columns)] * pairs + [(two, columns)] * pairs,
        "h" * 8,
        [pltpu.SemaphoreType.DMA((6 * pairs,))],
    )(
        *(
            pltpu.with_memory_space_constraint(array, pltpu.HBM)
            for array in (
                down_real,
                down_imaginary,
                up_real,
                up_imaginary,
                slowness,
                reflectivity,
                source_real,
                source_imaginary,
            )
        )
    )

    def exchanged(pieces):
        moved = [pieces[0]]
        for step in range(1, pairs):
            moved.append(lax.ppermute(pieces[step], "lat", across(step)))
        return moved

    planes = exchanged(outs[:pairs])
    media = exchanged(outs[pairs:])

    def factor_body(ref_slow, out, ref):
        here = Place(pairs)
        value = ref_slow[here.level]
        out[:tall], out[tall:] = multiplier(value, rows, columns, here.core)
        ref[...] = jnp.full((block, columns), value, f32)

    mult, ref_here = local_call(factor_body, [local, (block, columns)], "s")(
        ref_slow
    )

    def media_body(*refs):
        pieces, (ref, corr, refl) = refs[:pairs], refs[pairs:]
        here = Place(pairs)
        for step in range(pairs):
            start = (here.pair ^ step) * block
            theta = (pieces[step][pl.ds(0, block), :] - ref[...]) * (OMEGA * DEPTH_STEP)
            cosine, sine = cos_sin(theta)
            corr[pl.ds(pl.multiple_of(start, block), block), :] = cosine
            corr[pl.ds(pl.multiple_of(tall + start, block), block), :] = sine
            refl[pl.ds(pl.multiple_of(start, block), block), :] = pieces[step][
                pl.ds(block, block), :
            ]

    corr, refl = local_call(media_body, [local, (tall, columns)], "v" * pairs + "v")(
        *media, ref_here
    )

    def shared(first, second, here, keep, send):
        def put(mine, theirs):
            keep[:tall], keep[tall:] = mine
            send[:tall], send[tall:] = theirs

        @pl.when(here.core == 0)
        def _():
            put(first, second)

        @pl.when(here.core == 1)
        def _():
            put(second, first)

    def enter(which):
        def body(*refs):
            pieces, (table, turn, keep, send, whole) = refs[:pairs], refs[pairs:]
            here = Place(pairs)
            for step in range(pairs):
                start = (here.pair ^ step) * block
                for n in range(2):
                    whole[pl.ds(pl.multiple_of(n * tall + start, block), block), :] = pieces[step][
                        pl.ds((2 * which + n) * block, block), :
                    ]
            shared(*forward_y(whole[:tall], whole[tall:], table, turn), here, keep, send)

        outs, scratch = [part, part], [pltpu.VMEM(local, f32)]
        if which == 1:
            outs, scratch = outs + [local], []
        return local_call(body, outs, "v" * (pairs + 2), scratch)(
            *planes, y_table, y_turn
        )

    def mixed(which, ahead, behind, source):
        def body(ahead, behind, source, refl, table, turn, keep, send):
            here = Place(pairs)
            sign = jnp.where((here.level % 2 == 0) == (which == 0), -1.0, 1.0)
            behind = jnp.where(top(here), source[...], behind[...])
            base, side = (behind, ahead[...]) if which == 0 else (ahead[...], behind)
            weight = refl[...] * sign
            real = base[:tall] + weight * side[:tall]
            imag = base[tall:] + weight * side[tall:]
            shared(*forward_y(real, imag, table, turn), here, keep, send)

        return local_call(body, [part, part], "v" * 6)(ahead, behind, source, refl, y_table, y_turn)

    def column(keep, got):
        def body(keep, got, mult, table, back, turn, out, send, near, far):
            here = Place(pairs)
            for piece, core in ((keep, here.core), (got, 1 - here.core)):
                for n in range(2):
                    take = pl.ds(pl.multiple_of(n * tall + core * quarter, quarter), quarter)
                    near[take, :] = piece[pl.ds(n * tall, quarter), :]
                    far[take, :] = piece[pl.ds(n * tall + quarter, quarter), :]
            cosine, sine = turn[0], turn[1]
            d_real, d_imag = near[:tall] - far[:tall], near[tall:] - far[tall:]
            a = jnp.concatenate(
                [near[:tall] + far[:tall], d_real * cosine + d_imag * sine], axis=1
            )
            b = jnp.concatenate(
                [near[tall:] + far[tall:], d_imag * cosine - d_real * sine], axis=1
            )
            spec = jnp.dot(table[...], parts_of(a, b, 0), preferred_element_type=f32)
            a = spec[:tall] * mult[:tall] - spec[tall:] * mult[tall:]
            b = spec[:tall] * mult[tall:] + spec[tall:] * mult[:tall]
            moved = jnp.dot(back[...], parts_of(a, b, 0), preferred_element_type=f32)
            o_real, o_imag = moved[:tall, wide:], moved[tall:, wide:]
            o_real, o_imag = o_real * cosine - o_imag * sine, o_imag * cosine + o_real * sine
            e_real, e_imag = moved[:tall, :wide], moved[tall:, :wide]
            joined = []
            for even, odd in ((e_real, o_real), (e_imag, o_imag)):
                low, high = even + odd, even - odd
                joined.append(
                    [
                        jnp.concatenate([low[take], high[take]], axis=0)
                        for take in (slice(0, quarter), slice(quarter, tall))
                    ]
                )
            shared(*zip(*joined), here, out, send)

        return local_call(
            body, [part, part], "v" * 6, [pltpu.VMEM(part, f32) for _ in range(2)]
        )(keep, got, mult, x_table, x_back, x_turn)

    def corrected(keep, got, corr, table, turn, here, whole):
        for piece, core in ((keep, here.core), (got, 1 - here.core)):
            take = pl.ds(pl.multiple_of(core * tall, tall), tall)
            whole[take, pl.ds(0, wide)] = piece[:tall]
            whole[take, pl.ds(wide, wide)] = piece[tall:]
        real, imag = inverse_y(whole[:, :wide], whole[:, wide:], table, turn)
        cosine, sine = corr[:tall], corr[tall:]
        return real * cosine + imag * sine, imag * cosine - real * sine

    def leave(keep, got):
        def body(keep, got, corr, table, turn, out, whole):
            real, imag = corrected(keep, got, corr, table, turn, Place(pairs), whole)
            out[:tall], out[tall:] = real, imag

        return local_call(body, [local], "v" * 5, [pltpu.VMEM(local, f32)])(
            keep, got, corr, y_back, y_turn
        )[0]

    def leave_last(keep, got):
        def body(keep, got, corr, table, turn, *refs):
            outs, whole = refs[:pairs], refs[pairs]
            here = Place(pairs)
            real, imag = corrected(keep, got, corr, table, turn, here, whole)
            whole[:tall], whole[tall:] = real, imag
            for step in range(pairs):
                start = (here.pair ^ step) * block
                for m in range(2):
                    outs[step][pl.ds(m * block, block), :] = whole[
                        pl.ds(pl.multiple_of(m * tall + start, block), block), :
                    ]

        return local_call(
            body, [(two, columns)] * pairs, "v" * 5, [pltpu.VMEM(local, f32)]
        )(keep, got, corr, y_back, y_turn)

    def crossed(value):
        return lax.ppermute(value, "lat", swap)

    keep0, send0 = enter(0)
    got0 = crossed(send0)
    keep1, send1, source = enter(1)
    got1 = crossed(send1)
    for _ in range(TICKS - 1):
        keep0, send0 = column(keep0, got0)
        got0 = crossed(send0)
        keep1, send1 = column(keep1, got1)
        got1 = crossed(send1)
        first = leave(keep0, got0)
        ahead = lax.ppermute(first, ("depth", "lat"), level_pairs(sections, pairs, 0))
        second = leave(keep1, got1)
        behind = lax.ppermute(second, ("depth", "lat"), level_pairs(sections, pairs, 1))
        keep1, send1 = mixed(1, ahead, behind, source)
        got1 = crossed(send1)
        keep0, send0 = mixed(0, ahead, behind, source)
        got0 = crossed(send0)
    keep1, send1 = column(keep1, got1)
    got1 = crossed(send1)
    keep0, send0 = column(keep0, got0)
    got0 = crossed(send0)
    back1 = exchanged(leave_last(keep1, got1))
    leaving = leave_last(keep0, got0)
    back0 = exchanged(leaving)

    def pick_body(*refs):
        pieces, even, odd = refs[:pairs], refs[pairs], refs[pairs + 1]
        here = Place(pairs)
        for step in range(pairs):
            level = place_on(here.section, here.pair ^ step, pairs)
            for edge, mine in ((pairs - 1, 0), (0, 1)):
                for target, parity in ((even, mine), (odd, 1 - mine)):

                    @pl.when((level == edge) & (here.section % 2 == parity))
                    def _():
                        target[...] = pieces[step][...]

    even, odd = local_call(pick_body, [(two, columns)] * 2, "v" * pairs)(*back1)
    even = lax.ppermute(even, ("depth", "lat"), section_pairs(sections, pairs, 0))
    odd = lax.ppermute(odd, ("depth", "lat"), section_pairs(sections, pairs, 1))

    def mix_body(*refs):
        first, second = refs[:pairs], refs[pairs : 2 * pairs]
        even, odd, refl, sr, si = refs[2 * pairs : 2 * pairs + 5]
        dr, di, ur, ui, down, up = refs[2 * pairs + 5 :]
        here = Place(pairs)
        for step in range(pairs):
            level = place_on(here.section, here.pair ^ step, pairs)
            below, above = (level + 1) % levels, (level + levels - 1) % levels

            @pl.when(level % 2 == 0)
            def _():
                down[below] = first[step][...]
                up[above] = second[step][...]

            @pl.when(level % 2 == 1)
            def _():
                down[below] = second[step][...]
                up[above] = first[step][...]

        @pl.when(here.section % 2 == 0)
        def _():
            down[0] = odd[...]
            up[levels - 1] = even[...]

        @pl.when(here.section % 2 == 1)
        def _():
            down[0] = even[...]
            up[levels - 1] = odd[...]

        @pl.when(here.section == 0)
        def _():
            down[0, pl.ds(0, block), :] = sr[...]
            down[0, pl.ds(block, block), :] = si[...]

        for n in range(levels):
            r = refl[n]
            d_real, d_imag = down[n, pl.ds(0, block), :], down[n, pl.ds(block, block), :]
            u_real, u_imag = up[n, pl.ds(0, block), :], up[n, pl.ds(block, block), :]
            dr[n] = d_real - r * u_real
            di[n] = d_imag - r * u_imag
            ur[n] = u_real + r * d_real
            ui[n] = u_imag + r * d_imag

    return tuple(
        local_call(
            mix_body,
            [(levels, block, columns)] * 4,
            "v" * (2 * pairs + 5),
            [pltpu.VMEM((levels, two, columns), f32) for _ in range(2)],
        )(*back0, *back1, even, odd, reflectivity, source_real, source_imaginary)
    )


def fits(shape, mesh):
    levels, rows, columns = shape
    levels = levels // mesh.shape["depth"]
    return (
        mesh.shape["lat"] == 2 * levels
        and levels >= 2
        and levels & (levels - 1) == 0
        and rows // mesh.shape["lat"] % 16 == 0
        and columns % 256 == 0
    )


def solution(mesh):
    rows = P("depth", "lat", None)
    placed = (rows,) * 5 + (P("depth"), rows, P("lat", None), P("lat", None))

    def mapped(body):
        return jax.shard_map(
            body, mesh=mesh, in_specs=placed, out_specs=(rows,) * 4, check_vma=False
        )

    by_planes = mapped(plane_shards)
    by_rows = mapped(row_shards)

    def run(*arrays):
        return (by_planes if fits(arrays[0].shape, mesh) else by_rows)(*arrays)

    return run
```

```python
import math

import jax
import jax.numpy as jnp
import numpy as np
from jax import lax
from jax.experimental import pallas as pl
from jax.experimental.pallas import tpu as pltpu
from jax.sharding import PartitionSpec as P


TICKS = 3

OMEGA = 2.5
DEPTH_STEP = 1.0


def passed_along(value, axis, steps):
    count = lax.axis_size(axis)
    initial, last = (max(0, -steps), min(count, count - steps))
    return lax.ppermute(value, axis, [(source, source + steps) for source in range(initial, last)])


def tables(count):
    index = jnp.arange(count, dtype=jnp.int32)
    phase = index[:, None] * index[None, :] % count
    angle = phase.astype(jnp.float32) * (2.0 * math.pi / count)
    return (jnp.cos(angle), jnp.sin(angle))


def wrapped_numbers(index, count):
    folded = jnp.where(index < count // 2, index, index - count)
    return folded.astype(jnp.float32) * (2.0 * math.pi / count)


def complex_product(form, real, imag, cosine, sine, inverse):
    real_cos = jnp.einsum(form, real, cosine, precision=lax.Precision.HIGHEST)
    real_sin = jnp.einsum(form, real, sine, precision=lax.Precision.HIGHEST)
    imag_cos = jnp.einsum(form, imag, cosine, precision=lax.Precision.HIGHEST)
    imag_sin = jnp.einsum(form, imag, sine, precision=lax.Precision.HIGHEST)
    if inverse:
        return (real_cos - imag_sin, imag_cos + real_sin)
    return (real_cos + imag_sin, imag_cos - real_sin)


def spectral(real, imag, mult_real, mult_imag, corr_real, corr_imag, all_tables, lat_count):
    cos_y, sin_y, cos_x, sin_x = all_tables
    planes = real.shape[0]
    rows_here = real.shape[1]
    width_y = real.shape[2]
    width_x = rows_here * lat_count
    cols_here = width_y // lat_count
    first_real, first_imag = complex_product("nxy,yk->xkn", real, imag, cos_y, sin_y, False)
    send_real = jnp.swapaxes(
        first_real.reshape(rows_here, lat_count, cols_here, planes), 0, 1
    ).reshape(lat_count, rows_here * cols_here * planes)
    send_imag = jnp.swapaxes(
        first_imag.reshape(rows_here, lat_count, cols_here, planes), 0, 1
    ).reshape(lat_count, rows_here * cols_here * planes)
    got_real, got_imag = (
        lax.all_to_all(send_real, "lat", split_axis=0, concat_axis=0, tiled=True),
        lax.all_to_all(send_imag, "lat", split_axis=0, concat_axis=0, tiled=True),
    )
    got_real = got_real.reshape(width_x, cols_here, planes)
    got_imag = got_imag.reshape(width_x, cols_here, planes)
    spec_real, spec_imag = complex_product("xqn,xp->nqp", got_real, got_imag, cos_x, sin_x, False)
    moved_real = spec_real * mult_real - spec_imag * mult_imag
    moved_imag = spec_real * mult_imag + spec_imag * mult_real
    back_real, back_imag = complex_product(
        "nqp,px->qxn", moved_real, moved_imag, cos_x, sin_x, True
    )
    back_real = jnp.swapaxes(
        (back_real / width_x).reshape(cols_here, lat_count, rows_here, planes), 0, 1
    ).reshape(lat_count, cols_here * rows_here * planes)
    back_imag = jnp.swapaxes(
        (back_imag / width_x).reshape(cols_here, lat_count, rows_here, planes), 0, 1
    ).reshape(lat_count, cols_here * rows_here * planes)
    ret_real, ret_imag = (
        lax.all_to_all(back_real, "lat", split_axis=0, concat_axis=0, tiled=True),
        lax.all_to_all(back_imag, "lat", split_axis=0, concat_axis=0, tiled=True),
    )
    ret_real = ret_real.reshape(width_y, rows_here, planes)
    ret_imag = ret_imag.reshape(width_y, rows_here, planes)
    plane_real, plane_imag = complex_product("kxn,ky->nxy", ret_real, ret_imag, cos_y, sin_y, True)
    plane_real = plane_real / width_y
    plane_imag = plane_imag / width_y
    final_real = plane_real * corr_real - plane_imag * corr_imag
    final_imag = plane_real * corr_imag + plane_imag * corr_real
    return (final_real, final_imag)


def media_factors(slow_planes, slow_refs, lat_count, lat_index):
    rows_here = slow_planes.shape[1]
    width_y = slow_planes.shape[2]
    width_x = rows_here * lat_count
    cols_here = width_y // lat_count
    wave_x = wrapped_numbers(jnp.arange(width_x, dtype=jnp.int32), width_x)
    wave_y = wrapped_numbers(
        lat_index * cols_here + jnp.arange(cols_here, dtype=jnp.int32), width_y
    )
    squared = wave_y[:, None] ** 2 + wave_x[None, :] ** 2
    argument = (OMEGA * slow_refs[:, None, None]) ** 2 - squared[None]
    vertical = jnp.sqrt(jnp.maximum(argument, 0.0)) * DEPTH_STEP
    evanescent = jnp.sqrt(jnp.maximum(-argument, 0.0)) * DEPTH_STEP
    factor = jnp.exp(-evanescent)
    theta = OMEGA * (slow_planes - slow_refs[:, None, None]) * DEPTH_STEP
    return (
        factor * jnp.cos(vertical),
        -factor * jnp.sin(vertical),
        jnp.cos(theta),
        -jnp.sin(theta),
    )


def row_shards(
    down_real,
    down_imaginary,
    up_real,
    up_imaginary,
    slowness,
    ref_slow,
    reflectivity,
    source_real,
    source_imaginary,
):
    levels = down_real.shape[0]
    lat_count = lax.axis_size("lat")
    lat_index = lax.axis_index("lat")
    top_mask = (lax.axis_index("depth") == 0).astype(jnp.float32)
    width_x = down_real.shape[1] * lat_count
    cos_y, sin_y = tables(down_real.shape[2])
    cos_x, sin_x = tables(width_x)
    all_tables = (cos_y, sin_y, cos_x, sin_x)
    slow_planes = jnp.concatenate([slowness, slowness], axis=0)
    slow_refs = jnp.concatenate([ref_slow, ref_slow], axis=0)
    mult_real, mult_imag, corr_real, corr_imag = media_factors(
        slow_planes, slow_refs, lat_count, lat_index
    )
    for _ in range(TICKS):
        joined_real = jnp.concatenate([down_real, up_real], axis=0)
        joined_imag = jnp.concatenate([down_imaginary, up_imaginary], axis=0)
        prop_real, prop_imag = spectral(
            joined_real,
            joined_imag,
            mult_real,
            mult_imag,
            corr_real,
            corr_imag,
            all_tables,
            lat_count,
        )
        above_real, above_imag = passed_along(
            (prop_real[levels - 1], prop_imag[levels - 1]), "depth", 1
        )
        below_real, below_imag = passed_along((prop_real[levels], prop_imag[levels]), "depth", -1)
        head_real = above_real + top_mask * source_real
        head_imag = above_imag + top_mask * source_imaginary
        in_down_real = jnp.concatenate([head_real[None], prop_real[: levels - 1]], axis=0)
        in_down_imag = jnp.concatenate([head_imag[None], prop_imag[: levels - 1]], axis=0)
        in_up_real = jnp.concatenate([prop_real[levels + 1 :], below_real[None]], axis=0)
        in_up_imag = jnp.concatenate([prop_imag[levels + 1 :], below_imag[None]], axis=0)
        down_real = in_down_real - reflectivity * in_up_real
        down_imaginary = in_down_imag - reflectivity * in_up_imag
        up_real = in_up_real + reflectivity * in_down_real
        up_imaginary = in_up_imag + reflectivity * in_down_imag
    return (down_real, down_imaginary, up_real, up_imaginary)


def path_at(section, place, pairs):
    place = place if section % 2 == 0 else pairs - 1 - place
    return place ^ (place >> 1)


def place_on(section, pair, pairs):
    shift, place = 1, pair
    while (1 << shift) <= pairs:
        place = place ^ (pair >> shift)
        shift += 1
    return jnp.where(section % 2 == 0, place, pairs - 1 - place)


def level_pairs(sections, pairs, parity):
    where = [
        g * pairs * 2 + path_at(g, l, pairs) * 2 for g in range(sections) for l in range(pairs)
    ]
    edges = []
    for z in range(parity, len(where) - 1, 2):
        for core in range(2):
            here, below = where[z] + core, where[z + 1] + core
            edges += [(here, below), (below, here)]
    return edges


def section_pairs(sections, pairs, parity):
    width = 2 * pairs
    edges = []
    for g in range(parity, sections - 1, 2):
        for n in range(width):
            edges += [(g * width + n, (g + 1) * width + n), ((g + 1) * width + n, g * width + n)]
    return edges


def split_table(table):
    high = table.astype(np.float32).astype(jnp.bfloat16)
    return high, (table - high.astype(np.float64)).astype(np.float32).astype(jnp.bfloat16)


def half_tables(order, inverse):
    count = len(order)
    angle = (np.arange(count)[None, :] * np.asarray(order)[:, None] % count) * (
        2.0 * math.pi / count
    )
    if inverse:
        angle = angle.T
    (cos_high, cos_low), (sin_high, sin_low) = split_table(np.cos(angle)), split_table(
        np.sin(angle) * (-1.0 if inverse else 1.0)
    )
    real = [np.concatenate([c, -s], axis=1) for c, s in ((cos_high, sin_high), (cos_low, sin_low))]
    imag = [np.concatenate([s, c], axis=1) for c, s in ((cos_high, sin_high), (cos_low, sin_low))]
    return np.concatenate([real[0], real[0], real[1], imag[0], imag[0], imag[1]], axis=0)


def turn_tables(order):
    angle = np.asarray(order) * (math.pi / len(order))
    return np.stack([np.cos(angle), np.sin(angle)]).astype(np.float32)


def halves(value):
    high = value.astype(jnp.bfloat16)
    low = (value - high.astype(jnp.float32)).astype(jnp.bfloat16)
    return high, low


def cos_sin(angle):
    square = angle * angle
    sine = 1.0
    for n in (13, 11, 9, 7, 5, 3):
        scale = -1.0 / (n * (n - 1))
        sine = 1.0 + square * (scale * sine)
    cosine = 1.0
    for n in (14, 12, 10, 8, 6, 4, 2):
        scale = -1.0 / (n * (n - 1))
        cosine = 1.0 + square * (scale * cosine)
    return cosine, angle * sine


def multiplier(ref, rows, columns, core):
    shape = (rows // 2, columns)
    along = lax.broadcasted_iota(jnp.int32, shape, 1)
    odd = (along >= columns // 2).astype(jnp.int32)

    def wave(count, index):
        folded = jnp.where(index < count // 2, index, index - count)
        return folded.astype(jnp.float32) * (2.0 * math.pi / count)

    wave_x = wave(rows, 2 * lax.broadcasted_iota(jnp.int32, shape, 0) + odd)
    wave_y = wave(columns, 2 * (along - odd * (columns // 2)) + core)
    argument = (OMEGA * ref) ** 2 - (wave_x * wave_x + wave_y * wave_y)
    vertical = jnp.sqrt(jnp.maximum(argument, 0.0)) * DEPTH_STEP
    evanescent = jnp.sqrt(jnp.maximum(-argument, 0.0)) * DEPTH_STEP
    factor = jnp.exp(-evanescent) * (1.0 / (rows * columns))
    cosine, sine = cos_sin(0.5 * vertical)
    return factor * (1.0 - 2.0 * sine * sine), factor * (-2.0 * sine * cosine)


def parts_of(a, b, axis):
    a_high, a_low = halves(a)
    b_high, b_low = halves(b)
    return jnp.concatenate([a_high, a_low, a_high, b_high, b_low, b_high], axis=axis)


def forward_y(real, imag, table, turn):
    count, wide = real.shape[0], real.shape[1] // 2
    cosine, sine = turn[0:1, :], turn[1:2, :]
    d_real, d_imag = real[:, :wide] - real[:, wide:], imag[:, :wide] - imag[:, wide:]
    a = jnp.concatenate(
        [real[:, :wide] + real[:, wide:], d_real * cosine + d_imag * sine], axis=0
    )
    b = jnp.concatenate(
        [imag[:, :wide] + imag[:, wide:], d_imag * cosine - d_real * sine], axis=0
    )
    out = jnp.dot(parts_of(a, b, 1), table[...], preferred_element_type=jnp.float32)
    return (out[:count, :wide], out[:count, wide:]), (out[count:, :wide], out[count:, wide:])


def inverse_y(a, b, table, turn):
    count, wide = a.shape[0] // 2, a.shape[1]
    cosine, sine = turn[0:1, :], turn[1:2, :]
    out = jnp.dot(parts_of(a, b, 1), table[...], preferred_element_type=jnp.float32)
    e_real, e_imag = out[:count, :wide], out[:count, wide:]
    o_real, o_imag = out[count:, :wide], out[count:, wide:]
    o_real, o_imag = o_real * cosine - o_imag * sine, o_imag * cosine + o_real * sine
    return (
        jnp.concatenate([e_real + o_real, e_real - o_real], axis=1),
        jnp.concatenate([e_imag + o_imag, e_imag - o_imag], axis=1),
    )


class Place:
    def __init__(self, pairs):
        index = lax.axis_index("lat")
        self.section = lax.axis_index("depth")
        self.pair = index // 2
        self.core = index % 2
        self.level = place_on(self.section, self.pair, pairs)
        self.first = self.level == 0
        self.last = self.level == pairs - 1


def local_call(body, out_shapes, spaces, scratch=(), limit=24 << 20):
    memory = {"v": pltpu.VMEM, "s": pltpu.SMEM, "h": pltpu.HBM}
    return pl.pallas_call(
        body,
        out_shape=[
            jax.ShapeDtypeStruct(shape, jnp.float32) if isinstance(shape, tuple) else shape
            for shape in out_shapes
        ],
        in_specs=[pl.BlockSpec(memory_space=memory[space]) for space in spaces],
        out_specs=[pl.BlockSpec(memory_space=pltpu.VMEM) for _ in out_shapes],
        scratch_shapes=list(scratch),
        compiler_params=pltpu.CompilerParams(vmem_limit_bytes=limit),
    )


def plane_shards(
    down_real,
    down_imaginary,
    up_real,
    up_imaginary,
    slowness,
    ref_slow,
    reflectivity,
    source_real,
    source_imaginary,
):
    levels, block, columns = down_real.shape
    sections = lax.axis_size("depth")
    lat_count = lax.axis_size("lat")
    pairs = lat_count // 2
    rows = block * lat_count
    tall = rows // 2
    wide = columns // 2
    two, four = 2 * block, 4 * block
    swap = [(index, index ^ 1) for index in range(lat_count)]
    quarter = tall // 2
    place = np.arange(tall)
    order = place % quarter // block * two + place // quarter * block + place % block
    straight = np.arange(wide)
    y_table, y_back = (jnp.asarray(half_tables(straight, inverse)) for inverse in (False, True))
    x_table, x_back = (jnp.asarray(half_tables(order, inverse).T) for inverse in (False, True))
    y_turn = jnp.asarray(turn_tables(straight))
    x_turn = jnp.asarray(
        np.broadcast_to(turn_tables(order)[:, :, None], (2, tall, wide)).copy()
    )
    f32 = jnp.float32
    local = (2 * tall, columns)
    part = (2 * tall, wide)

    def across(step):
        return [(index, index ^ (2 * step)) for index in range(lat_count)]

    def top(here):
        return here.first & (here.section == 0)

    def split_body(dr, di, ur, ui, slow, refl, sr, si, *rest):
        planes, media, sems = rest[:pairs], rest[pairs : 2 * pairs], rest[2 * pairs]
        here = Place(pairs)

        def pieces(step, first, second):
            level = place_on(here.section, here.pair ^ step, pairs)
            out = []
            for n, array in enumerate(first + second):
                source = array if len(array.shape) == 2 else array.at[level]
                out.append((source, planes[step].at[pl.ds(n * block, block), :]))
            out.append((slow.at[level], media[step].at[pl.ds(0, block), :]))
            out.append((refl.at[level], media[step].at[pl.ds(block, block), :]))
            return [
                pltpu.make_async_copy(source, target, sems.at[step * 6 + n])
                for n, (source, target) in enumerate(out)
            ]

        def each(act):
            for step in range(pairs):
                level = place_on(here.section, here.pair ^ step, pairs)
                sourced = (level == 0) & (here.section == 0)

                @pl.when(sourced)
                def _():
                    for move in pieces(step, (sr, si), (dr, di)):
                        act(move)

                @pl.when((level % 2 == 0) & jnp.logical_not(sourced))
                def _():
                    for move in pieces(step, (ur, ui), (dr, di)):
                        act(move)

                @pl.when(level % 2 == 1)
                def _():
                    for move in pieces(step, (dr, di), (ur, ui)):
                        act(move)

        each(lambda move: move.start())
        each(lambda move: move.wait())

    outs = local_call(
        split_body,
        [(four, columns)] * pairs + [(two, columns)] * pairs,
        "h" * 8,
        [pltpu.SemaphoreType.DMA((6 * pairs,))],
    )(
        *(
            pltpu.with_memory_space_constraint(array, pltpu.HBM)
            for array in (
                down_real,
                down_imaginary,
                up_real,
                up_imaginary,
                slowness,
                reflectivity,
                source_real,
                source_imaginary,
            )
        )
    )

    def exchanged(pieces):
        moved = list(pieces)
        for step in range(1, pairs):
            moved[step] = lax.ppermute(pieces[step], "lat", across(step))
        return moved

    planes = exchanged(outs[:pairs])
    media = exchanged(outs[pairs:])

    def factor_body(ref_slow, out, ref):
        here = Place(pairs)
        value = ref_slow[here.level]
        out[:tall], out[tall:] = multiplier(value, rows, columns, here.core)
        ref[...] = jnp.full((block, columns), value, f32)

    mult, ref_here = local_call(factor_body, [local, (block, columns)], "s")(
        ref_slow
    )

    def media_body(*refs):
        pieces, (ref, corr, refl) = refs[:pairs], refs[pairs:]
        here = Place(pairs)
        for step in range(pairs):
            start = (here.pair ^ step) * block
            theta = (pieces[step][pl.ds(0, block), :] - ref[...]) * (OMEGA * DEPTH_STEP)
            cosine, sine = cos_sin(theta)
            corr[pl.ds(pl.multiple_of(start, block), block), :] = cosine
            corr[pl.ds(pl.multiple_of(tall + start, block), block), :] = sine
            refl[pl.ds(pl.multiple_of(start, block), block), :] = pieces[step][
                pl.ds(block, block), :
            ]

    corr, refl = local_call(media_body, [local, (tall, columns)], "v" * pairs + "v")(
        *media, ref_here
    )

    def shared(first, second, here, keep, send):
        def put(mine, theirs):
            keep[:tall], keep[tall:] = mine
            send[:tall], send[tall:] = theirs

        @pl.when(here.core == 0)
        def _():
            put(first, second)

        @pl.when(here.core == 1)
        def _():
            put(second, first)

    def enter(which):
        def body(*refs):
            pieces, (table, turn, keep, send, whole) = refs[:pairs], refs[pairs:]
            here = Place(pairs)
            for step in range(pairs):
                start = (here.pair ^ step) * block
                for n in range(2):
                    whole[pl.ds(pl.multiple_of(n * tall + start, block), block), :] = pieces[step][
                        pl.ds((2 * which + n) * block, block), :
                    ]
            shared(*forward_y(whole[:tall], whole[tall:], table, turn), here, keep, send)

        outs, scratch = [part, part], [pltpu.VMEM(local, f32)]
        if which == 0:
            outs, scratch = outs + [local], []
        return local_call(body, outs, "v" * (pairs + 2), scratch)(
            *planes, y_table, y_turn
        )

    def mixed(which, ahead, behind, source):
        def body(ahead, behind, source, refl, table, turn, keep, send):
            here = Place(pairs)
            sign = jnp.where((here.level % 2 == 0) == (which == 0), 1.0, -1.0)
            ahead = jnp.where(top(here), source[...], ahead[...])
            base, side = (behind[...], ahead) if which == 0 else (ahead, behind[...])
            weight = refl[...] * sign
            real = base[:tall] + weight * side[:tall]
            imag = base[tall:] + weight * side[tall:]
            shared(*forward_y(real, imag, table, turn), here, keep, send)

        return local_call(body, [part, part], "v" * 6)(ahead, behind, source, refl, y_table, y_turn)

    def column(keep, got):
        def body(keep, got, mult, table, back, turn, out, send, near, far):
            here = Place(pairs)
            for piece, core in ((keep, here.core), (got, 1 - here.core)):
                for n in range(2):
                    take = pl.ds(pl.multiple_of(n * tall + core * quarter, quarter), quarter)
                    near[take, :] = piece[pl.ds(n * tall, quarter), :]
                    far[take, :] = piece[pl.ds(n * tall + quarter, quarter), :]
            cosine, sine = turn[0], turn[1]
            d_real, d_imag = near[:tall] - far[:tall], near[tall:] - far[tall:]
            a = jnp.concatenate(
                [near[:tall] + far[:tall], d_real * cosine + d_imag * sine], axis=1
            )
            b = jnp.concatenate(
                [near[tall:] + far[tall:], d_imag * cosine - d_real * sine], axis=1
            )
            spec = jnp.dot(table[...], parts_of(a, b, 0), preferred_element_type=f32)
            a = spec[:tall] * mult[:tall] - spec[tall:] * mult[tall:]
            b = spec[:tall] * mult[tall:] + spec[tall:] * mult[:tall]
            moved = jnp.dot(back[...], parts_of(a, b, 0), preferred_element_type=f32)
            o_real, o_imag = moved[:tall, wide:], moved[tall:, wide:]
            o_real, o_imag = o_real * cosine - o_imag * sine, o_imag * cosine + o_real * sine
            e_real, e_imag = moved[:tall, :wide], moved[tall:, :wide]
            joined = []
            for even, odd in ((e_real, o_real), (e_imag, o_imag)):
                low, high = even + odd, even - odd
                joined.append(
                    [
                        jnp.concatenate([low[take], high[take]], axis=0)
                        for take in (slice(0, quarter), slice(quarter, tall))
                    ]
                )
            shared(*zip(*joined), here, out, send)

        return local_call(
            body, [part, part], "v" * 6, [pltpu.VMEM(part, f32) for _ in range(2)]
        )(keep, got, mult, x_table, x_back, x_turn)

    def corrected(keep, got, corr, table, turn, here, whole):
        for piece, core in ((keep, here.core), (got, 1 - here.core)):
            take = pl.ds(pl.multiple_of(core * tall, tall), tall)
            whole[take, pl.ds(0, wide)] = piece[:tall]
            whole[take, pl.ds(wide, wide)] = piece[tall:]
        real, imag = inverse_y(whole[:, :wide], whole[:, wide:], table, turn)
        cosine, sine = corr[:tall], corr[tall:]
        return real * cosine + imag * sine, imag * cosine - real * sine

    def leave(keep, got):
        def body(keep, got, corr, table, turn, out, whole):
            real, imag = corrected(keep, got, corr, table, turn, Place(pairs), whole)
            out[:tall], out[tall:] = real, imag

        return local_call(body, [local], "v" * 5, [pltpu.VMEM(local, f32)])(
            keep, got, corr, y_back, y_turn
        )[0]

    def leave_last(keep, got):
        def body(keep, got, corr, table, turn, *refs):
            outs, whole = refs[:pairs], refs[pairs]
            here = Place(pairs)
            real, imag = corrected(keep, got, corr, table, turn, here, whole)
            whole[:tall], whole[tall:] = real, imag
            for step in range(pairs):
                start = (here.pair ^ step) * block
                for m in range(2):
                    outs[step][pl.ds(m * block, block), :] = whole[
                        pl.ds(pl.multiple_of(m * tall + start, block), block), :
                    ]

        return local_call(
            body, [(two, columns)] * pairs, "v" * 5, [pltpu.VMEM(local, f32)]
        )(keep, got, corr, y_back, y_turn)

    def crossed(value):
        return lax.ppermute(value, "lat", swap)

    keep0, send0, source = enter(0)
    got0 = crossed(send0)
    keep1, send1 = enter(1)
    got1 = crossed(send1)
    for _ in range(TICKS - 1):
        keep0, send0 = column(keep0, got0)
        got0 = crossed(send0)
        keep1, send1 = column(keep1, got1)
        got1 = crossed(send1)
        first = leave(keep0, got0)
        ahead = lax.ppermute(first, ("depth", "lat"), level_pairs(sections, pairs, 1))
        second = leave(keep1, got1)
        behind = lax.ppermute(second, ("depth", "lat"), level_pairs(sections, pairs, 0))
        keep0, send0 = mixed(0, ahead, behind, source)
        got0 = crossed(send0)
        keep1, send1 = mixed(1, ahead, behind, source)
        got1 = crossed(send1)
    keep0, send0 = column(keep0, got0)
    got0 = crossed(send0)
    keep1, send1 = column(keep1, got1)
    got1 = crossed(send1)
    back0 = exchanged(leave_last(keep0, got0))
    back1 = exchanged(leave_last(keep1, got1))

    def pick_body(*refs):
        pieces, even, odd = refs[:pairs], refs[pairs], refs[pairs + 1]
        here = Place(pairs)
        for step in range(pairs):
            level = place_on(here.section, here.pair ^ step, pairs)
            for edge, mine in ((pairs - 1, 0), (0, 1)):
                for target, parity in ((even, mine), (odd, 1 - mine)):

                    @pl.when((level == edge) & (here.section % 2 == parity))
                    def _():
                        target[...] = pieces[step][...]

    even, odd = local_call(pick_body, [(two, columns)] * 2, "v" * pairs)(*back0)
    even = lax.ppermute(even, ("depth", "lat"), section_pairs(sections, pairs, 0))
    odd = lax.ppermute(odd, ("depth", "lat"), section_pairs(sections, pairs, 1))

    def mix_body(*refs):
        first, second = refs[:pairs], refs[pairs : 2 * pairs]
        even, odd, refl, sr, si = refs[2 * pairs : 2 * pairs + 5]
        dr, di, ur, ui, down, up = refs[2 * pairs + 5 :]
        here = Place(pairs)
        for step in range(pairs):
            level = place_on(here.section, here.pair ^ step, pairs)
            below, above = (level + 1) % levels, (level + levels - 1) % levels

            @pl.when(level % 2 == 0)
            def _():
                down[below] = second[step][...]
                up[above] = first[step][...]

            @pl.when(level % 2 == 1)
            def _():
                down[below] = first[step][...]
                up[above] = second[step][...]

        @pl.when(here.section % 2 == 0)
        def _():
            down[0] = odd[...]
            up[levels - 1] = even[...]

        @pl.when(here.section % 2 == 1)
        def _():
            down[0] = even[...]
            up[levels - 1] = odd[...]

        @pl.when(here.section == 0)
        def _():
            down[0, pl.ds(0, block), :] = sr[...]
            down[0, pl.ds(block, block), :] = si[...]

        for n in range(levels):
            r = refl[n]
            d_real, d_imag = down[n, pl.ds(0, block), :], down[n, pl.ds(block, block), :]
            u_real, u_imag = up[n, pl.ds(0, block), :], up[n, pl.ds(block, block), :]
            dr[n] = d_real - r * u_real
            di[n] = d_imag - r * u_imag
            ur[n] = u_real + r * d_real
            ui[n] = u_imag + r * d_imag

    return tuple(
        local_call(
            mix_body,
            [(levels, block, columns)] * 4,
            "v" * (2 * pairs + 5),
            [pltpu.VMEM((levels, two, columns), f32) for _ in range(2)],
        )(*back0, *back1, even, odd, reflectivity, source_real, source_imaginary)
    )


def fits(shape, mesh):
    levels, rows, columns = shape
    levels = levels // mesh.shape["depth"]
    return (
        mesh.shape["lat"] == 2 * levels
        and levels >= 2
        and levels & (levels - 1) == 0
        and rows // mesh.shape["lat"] % 16 == 0
        and columns % 256 == 0
    )


def solution(mesh):
    rows = P("depth", "lat", None)
    placed = (rows,) * 5 + (P("depth"), rows, P("lat", None), P("lat", None))

    def mapped(body):
        return jax.shard_map(
            body, mesh=mesh, in_specs=placed, out_specs=(rows,) * 4, check_vma=False
        )

    by_planes = mapped(plane_shards)
    by_rows = mapped(row_shards)

    def run(*arrays):
        return (by_planes if fits(arrays[0].shape, mesh) else by_rows)(*arrays)

    return run
```
